32 devices in a mesh: section: 2 (over y), dp: 4 (over x, core), mp: 4 (over z).
Axes of the slice: x: 2, y: 2, z: 4, core: 2. Of those that a mesh axis runs over, the one named last changes fastest.
Arguments:
- activations: bfloat16 [2, 256, 4096], P(None, 'dp'), may hold values from -6 to 6
- cotangent: bfloat16 [2, 256, 4096], P(None, 'dp'), may hold values from -6 to 6
- norm_gain: float32 [2, 4096], P('section'), may hold values from 0.1 to 1.9
- w_up: bfloat16 [2, 4096, 8192], P('section', 'dp', 'mp'), may hold values from -0.09375 to 0.09375
- w_down: bfloat16 [2, 4096, 8192], P('section', 'dp', 'mp'), may hold values from -0.0625 to 0.0625
- gram_left: float32 [2, 128, 512, 512], P('section', ('dp', 'mp')), as said below
- gram_right: float32 [2, 128, 512, 512], P('section', ('dp', 'mp')), as said below
- root_left: bfloat16 [2, 128, 512, 512], P('section', ('dp', 'mp'))
- root_right: bfloat16 [2, 128, 512, 512], P('section', ('dp', 'mp'))
- owner_slot: int32 [2, 16, 8], replicated, may hold values from 0 to 127, as said below
- eighth: int32 [2, 16, 8], replicated, may hold values from 0 to 7, as said below
- refresh_phase: int32 [1], replicated, may hold values from 0 to 999999
Outputs:
- new_gram_left: float32 [2, 128, 512, 512], P('section', ('dp', 'mp'))
- new_gram_right: float32 [2, 128, 512, 512], P('section', ('dp', 'mp'))
- new_root_left: bfloat16 [2, 128, 512, 512], P('section', ('dp', 'mp'))
- new_root_right: bfloat16 [2, 128, 512, 512], P('section', ('dp', 'mp'))
- update_blocks: bfloat16 [2, 128, 512, 512], P('section', ('dp', 'mp'))
The draws below stay inside these ranges and needn't reach their ends.
Inputs may be any that keep to these rules, and one draw needn't show every extreme that they name: `owner_slot`: for each section, a permutation of the 128 slots; the block of flat index f = i * 8 + j goes to a slot t with (t // 8) % (4) == f // 32. `eighth`: in each section and each run of 32 consecutive flat block indices, every value is taken by exactly 4 blocks. `gram_left`: symmetric positive definite. `gram_right`: symmetric positive definite.
All inputs are finite; a program needn't handle non-finite values.
Results may differ from the reference program's by a relative error of at most 0.025.
Values may be sent and summed in bfloat16 or wider, within the bound.
A program may use at most 192 MiB of HBM per device.

```python
import math
import jax
import jax.numpy as jnp
from jax import lax

D = 4096
FFW = 8192
BLK = 512
MB = 2
TOK_MB = 64
ITERS = 2
TOKENS_MB = 256
NROW = 16
NCOL = 8
SLOTS = 128
GROUP = 32
BPD = 8
N_SECTION = 2
N_DP = 4
N_MP = 4


def gram_draw(key, salt):
    inner_key = jax.random.fold_in(key, salt)
    draw_keys = jax.random.split(inner_key, 8)
    top_count = 3
    support_width = max(BLK // 32, 4)
    batch_count = N_SECTION * SLOTS * top_count
    support_keys = jax.random.split(draw_keys[0], batch_count)
    support = jax.vmap(lambda one_key: jax.random.permutation(one_key, BLK)[:support_width])(support_keys)
    onehot = (support[:, :, None] == jnp.arange(BLK, dtype=jnp.int32)[None, None, :]).astype(jnp.float32)
    sign_values = jnp.where(jax.random.bernoulli(draw_keys[1], 0.5, (batch_count, support_width)), 1.0, -1.0).astype(jnp.float32)
    magnitudes = jax.random.uniform(draw_keys[2], (batch_count, support_width), jnp.float32, 0.5, 1.5)
    ratios = jax.random.uniform(draw_keys[3], (N_SECTION, SLOTS, top_count - 1), jnp.float32, 0.3, 0.6)
    top_level = 40.0 * jax.random.uniform(draw_keys[4], (N_SECTION, SLOTS, 1), jnp.float32, 0.8, 1.2)
    factor = jax.random.uniform(draw_keys[5], (N_SECTION, SLOTS, BLK, BLK), jnp.float32, -1.0, 1.0) * math.sqrt(3.0)
    tail_decay = jnp.power(10.0, -3.0 * jax.random.uniform(draw_keys[6], (N_SECTION, SLOTS, BLK), jnp.float32))
    diagonal = jax.random.uniform(draw_keys[7], (N_SECTION, SLOTS, BLK), jnp.float32, 0.05, 0.2)
    entries = sign_values * magnitudes
    vectors = jnp.einsum('bw,bwn->bn', entries, onehot)
    vectors = vectors / jnp.sqrt(jnp.sum(vectors * vectors, axis=-1, keepdims=True))
    vectors = vectors.reshape(N_SECTION, SLOTS, top_count, BLK)
    strengths = top_level * jnp.concatenate([jnp.ones((N_SECTION, SLOTS, 1), jnp.float32), ratios], axis=-1)
    top_part = jnp.einsum('sbk,sbki,sbkj->sbij', strengths, vectors, vectors)
    tail_part = jnp.einsum('sbij,sbj,sbkj->sbik', factor, tail_decay, factor) / BLK
    matrix = top_part + tail_part + diagonal[..., None] * jnp.eye(BLK, dtype=jnp.float32)
    return 0.5 * (matrix + jnp.swapaxes(matrix, -1, -2))


def root_draw(key, salt):
    inner_key = jax.random.fold_in(key, salt)
    key_diag, key_noise = jax.random.split(inner_key, 2)
    diagonal = jax.random.uniform(key_diag, (N_SECTION, SLOTS, BLK), jnp.float32, 0.3, 0.8)
    noise_part = 0.01 * jax.random.normal(key_noise, (N_SECTION, SLOTS, BLK, BLK), jnp.float32)
    matrix = noise_part + diagonal[..., None] * jnp.eye(BLK, dtype=jnp.float32)
    return matrix.astype(jnp.bfloat16)


def group_shuffles(key, salt):
    group_keys = jax.random.split(jax.random.fold_in(key, salt), N_SECTION * N_MP)
    shuffles = jax.vmap(lambda one_key: jax.random.permutation(one_key, GROUP))(group_keys)
    return shuffles.reshape(N_SECTION, N_MP, GROUP).astype(jnp.int32)


def draw_gram_left(key, part):
    return gram_draw(key, 11)


def draw_gram_right(key, part):
    return gram_draw(key, 12)


def draw_root_left(key, part):
    return root_draw(key, 13)


def draw_root_right(key, part):
    return root_draw(key, 14)


def draw_owner_slot(key, part):
    shuffles = group_shuffles(key, 21)
    group_ids = jnp.arange(N_MP, dtype=jnp.int32)[None, :, None]
    slot_values = (shuffles // BPD * N_MP + group_ids) * BPD + shuffles % BPD
    return slot_values.reshape(N_SECTION, NROW, NCOL).astype(jnp.int32)


def draw_eighth(key, part):
    shuffles = group_shuffles(key, 22)
    return (shuffles % 8).reshape(N_SECTION, NROW, NCOL).astype(jnp.int32)


def block_levels(rng, extent, pieces, low, largest):
    factor_of, own = 1.0, jax.random.fold_in(rng, 6)
    for axis_at, blocks in pieces:
        steps = jnp.exp(jax.random.uniform(jax.random.fold_in(own, axis_at), (blocks,), jnp.float32, low / len(pieces), largest / len(pieces)))
        factor_of = factor_of * jnp.repeat(steps, extent[axis_at] // blocks).reshape([-1 if axis == axis_at else 1 for axis in range(len(extent))])
    return factor_of


def noise(rng, dims, scale, reach, cuts=(), kind=jnp.bfloat16):
    result = jax.random.normal(rng, dims, jnp.float32) * scale
    if len(cuts) > 0:
        result = block_levels(rng, dims, cuts, -0.22, 0.18) * result
    return jnp.clip(result, min=-reach, max=reach).astype(kind)


def setup_inputs(seed: int = 0) -> dict:
    key_of = jax.random.split(jax.random.key(seed), 13)
    activations = noise(key_of[0], (MB, TOKENS_MB, D), 1.0, 6.0, ((1, 4),))
    cotangent = noise(key_of[1], (MB, TOKENS_MB, D), 1.0, 6.0, ((1, 4),))
    norm_gain = jnp.clip(1.0 + 0.18 * jax.random.normal(key_of[2], (N_SECTION, D), jnp.float32), 0.1, 1.9)
    w_up = noise(key_of[3], (N_SECTION, D, FFW), D ** -0.5, 0.09375, ((0, 2), (1, 4), (2, 4)))
    w_down = noise(key_of[4], (N_SECTION, D, FFW), FFW ** -0.5, 0.0625, ((0, 2), (1, 4), (2, 4)))
    gram_left = draw_gram_left(jax.random.fold_in(key_of[12], 71), 0)
    gram_right = draw_gram_right(jax.random.fold_in(key_of[12], 71), 0)
    root_left = draw_root_left(jax.random.fold_in(key_of[12], 71), 0)
    root_right = draw_root_right(jax.random.fold_in(key_of[12], 71), 0)
    owner_slot = draw_owner_slot(jax.random.fold_in(key_of[12], 71), 0)
    eighth = draw_eighth(jax.random.fold_in(key_of[12], 71), 0)
    refresh_phase = jax.random.randint(key_of[11], (1,), 0, 1000000).astype(jnp.int32)
    return {"activations": activations, "cotangent": cotangent, "norm_gain": norm_gain, "w_up": w_up, "w_down": w_down, "gram_left": gram_left, "gram_right": gram_right, "root_left": root_left, "root_right": root_right, "owner_slot": owner_slot, "eighth": eighth, "refresh_phase": refresh_phase}


norm_epsilon = 1e-05
decay_rate = 0.9
ridge_shift = 0.001
highest = lax.Precision.HIGHEST

def normalize_values(values, gain_row):
    inverse_rms = lax.rsqrt(lax.optimization_barrier(jnp.mean(values * values, axis=-1, keepdims=True)) + norm_epsilon)
    return values * inverse_rms * gain_row

def silu_slope(pre_act):
    sigmoid_values = jax.nn.sigmoid(pre_act)
    return sigmoid_values * (1.0 + pre_act * (1.0 - sigmoid_values))

def inverse_root(matrix):
    matrix_order = matrix.shape[-1]
    identity = jnp.eye(matrix_order, dtype=jnp.float32)
    shifted = matrix + ridge_shift * identity
    factor = 2.5 / jnp.sqrt(jnp.sum(shifted * shifted))
    iterate = jnp.power(factor, 0.25) * identity
    moment = factor * shifted
    for sweep_no in range(ITERS):
        step_mat = 1.25 * identity - 0.25 * moment
        square = jnp.dot(step_mat, step_mat, precision=highest)
        fourth = jnp.dot(square, square, precision=highest)
        moment = jnp.dot(fourth, moment, precision=highest)
        iterate = jnp.dot(iterate, step_mat, precision=highest)
    return iterate

def split_sum(left_rows, right_rows):
    left_parts = jnp.moveaxis(left_rows.reshape(left_rows.shape[0], N_MP, -1), 1, 0)
    right_parts = jnp.moveaxis(right_rows.reshape(right_rows.shape[0], N_MP, -1), 1, 0)

    def add_part(running_total, pair_in):
        product = lax.dot_general(pair_in[0], pair_in[1], (((1,), (1,)), ((), ())), preferred_element_type=jnp.float32)
        rounded = lax.optimization_barrier(product.astype(jnp.bfloat16)).astype(jnp.float32)
        return (running_total + rounded, None)
    zero_sum = jnp.zeros((left_rows.shape[0], right_rows.shape[0]), jnp.float32)
    running_total, unused = lax.scan(add_part, zero_sum, (left_parts, right_parts))
    return running_total

def forward_layer(inputs, gain_row, up_rows, down_rows):
    values = inputs.astype(jnp.float32)
    normed = normalize_values(values, gain_row).astype(jnp.bfloat16)
    pre_act = jnp.dot(normed, up_rows, preferred_element_type=jnp.float32)
    hidden = jax.nn.silu(pre_act).astype(jnp.bfloat16)
    output = (values + split_sum(hidden, down_rows)).astype(jnp.bfloat16)
    return (output, pre_act, hidden)

def backward_layer(grad_output, inputs, pre_act, gain_row, up_rows, down_rows):
    grad_hidden = jnp.dot(grad_output, down_rows, preferred_element_type=jnp.float32)
    grad_pre = (grad_hidden * silu_slope(pre_act)).astype(jnp.bfloat16)
    grad_normed = split_sum(grad_pre, up_rows)
    values = inputs.astype(jnp.float32)
    unused, pullback = jax.vjp(lambda values_in: normalize_values(values_in, gain_row), values)
    grad_values = pullback(grad_normed)[0]
    return (grad_output.astype(jnp.float32) + grad_values).astype(jnp.bfloat16)

def reference(activations, cotangent, norm_gain, w_up, w_down, gram_left, gram_right, root_left, root_right, owner_slot, eighth, refresh_phase):
    section_total = w_up.shape[0]
    micro_count, token_rows, model_width = activations.shape
    flat_rows = micro_count * token_rows
    layer_in = activations.reshape(flat_rows, model_width)
    section_saved = []
    for section_no in range(section_total):
        output, pre_act, hidden = forward_layer(layer_in, norm_gain[section_no], w_up[section_no], w_down[section_no])
        section_saved.append((layer_in, pre_act, hidden))
        layer_in = output
    grad_output = cotangent.reshape(flat_rows, model_width)
    section_grads = [None] * section_total
    for section_no in reversed(range(section_total)):
        inputs, pre_act, hidden = section_saved[section_no]
        section_grads[section_no] = (hidden, grad_output)
        if section_no > 0:
            grad_output = backward_layer(grad_output, inputs, pre_act, norm_gain[section_no], w_up[section_no], w_down[section_no])
    phase_now = refresh_phase[0] % 8
    gram_lefts, gram_rights, root_lefts, root_rights, updates = ([], [], [], [], [])
    for section_no in range(section_total):
        hidden, grad_out = section_grads[section_no]
        hidden_rep = hidden.reshape(micro_count, N_DP, TOK_MB, FFW).transpose(1, 0, 2, 3).reshape(N_DP, micro_count * TOK_MB, FFW)
        grad_rep = grad_out.reshape(micro_count, N_DP, TOK_MB, model_width).transpose(1, 0, 2, 3).reshape(N_DP, micro_count * TOK_MB, model_width)

        def add_replica(running_total, pair_in):
            product = lax.dot_general(pair_in[0], pair_in[1], (((0,), (0,)), ((), ())), preferred_element_type=jnp.float32)
            rounded = lax.optimization_barrier(product.astype(jnp.bfloat16)).astype(jnp.float32)
            return (running_total + rounded, None)
        zero_sum = jnp.zeros((FFW, model_width), jnp.float32)
        summed, unused = lax.scan(add_replica, zero_sum, (hidden_rep, grad_rep))
        scaled = summed * (1.0 / math.sqrt(micro_count * token_rows))
        blocks = scaled.reshape(NROW, BLK, NCOL, BLK).transpose(0, 2, 1, 3).reshape(SLOTS, BLK, BLK)
        block_of_slot = jnp.argsort(owner_slot[section_no].reshape(-1)).astype(jnp.int32)
        slot_grad = blocks[block_of_slot]
        is_due = eighth[section_no].reshape(-1)[block_of_slot] == phase_now
        left_new = decay_rate * gram_left[section_no] + jnp.einsum('sij,skj->sik', slot_grad, slot_grad, precision=highest) / BLK
        right_new = decay_rate * gram_right[section_no] + jnp.einsum('sji,sjk->sik', slot_grad, slot_grad, precision=highest) / BLK
        due_slots = jnp.argsort(jnp.logical_not(is_due).astype(jnp.int32), stable=True)[:SLOTS // 8].astype(jnp.int32)
        fresh_left = jax.vmap(inverse_root)(left_new[due_slots]).astype(jnp.bfloat16)
        fresh_right = jax.vmap(inverse_root)(right_new[due_slots]).astype(jnp.bfloat16)
        roots_l = root_left[section_no].at[due_slots].set(fresh_left)
        roots_r = root_right[section_no].at[due_slots].set(fresh_right)
        grad_low = slot_grad.astype(jnp.bfloat16)
        inner_product = jnp.einsum('sij,sjk->sik', grad_low.astype(jnp.float32), roots_r.astype(jnp.float32), precision=highest).astype(jnp.bfloat16)
        update = jnp.einsum('sij,sjk->sik', roots_l.astype(jnp.float32), inner_product.astype(jnp.float32), precision=highest).astype(jnp.bfloat16)
        gram_lefts.append(left_new)
        gram_rights.append(right_new)
        root_lefts.append(roots_l)
        root_rights.append(roots_r)
        updates.append(update)
    return (jnp.stack(gram_lefts), jnp.stack(gram_rights), jnp.stack(root_lefts), jnp.stack(root_rights), jnp.stack(updates))
```

```python
import math

import jax
import jax.numpy as jnp
from jax import lax
from jax.experimental import pallas as pl
from jax.experimental.pallas import tpu as pltpu
from jax.sharding import PartitionSpec as P

BLK = 512
MESH = pl.DeviceIdType.MESH
VMEM_LIMIT = 60 * 1024 * 1024

norm_epsilon = 1e-05
decay_rate = 0.9
ridge_shift = 0.001


def meet(devices):
    barrier = pltpu.get_barrier_semaphore()
    for device in devices:
        pl.semaphore_signal(barrier, inc=1, device_id=device, device_id_type=MESH)
    pl.semaphore_wait(barrier, len(devices))


def chunks_of(rows, row_count):
    fits = lambda n: rows % n == 0 and row_count % (rows // n) == 0 and (rows // n) % 16 == 0
    return max([n for n in (1, 2, 4) if fits(n)])


def matmul(left, right, left_dim=1, right_dim=0):
    return lax.dot_general(
        left, right, (((left_dim,), (right_dim,)), ((), ())), preferred_element_type=jnp.float32
    )


def relay(activations, cotangent, gain_rows, w_up, w_down):
    micro_count, row_count, model = activations.shape
    width, ff = w_up.shape
    dp_count, mp_count = lax.axis_size("dp"), lax.axis_size("mp")
    chips = dp_count // 2
    hops = chips.bit_length() - 1
    rows = micro_count * row_count
    chunks = chunks_of(rows, row_count)
    sub = rows // chunks
    tall = sub * dp_count
    half, own = tall // 2, tall // mp_count
    ff_tile, out_tile = min(512, ff), min(256, width)
    low, f32 = jnp.bfloat16, jnp.float32

    families = {
        "swap": chunks * (dp_count - 1),
        "pair_a": chunks,
        "pair_b": chunks,
        "cross_a": chunks * hops,
        "cross_b": chunks * hops,
        "hidden": chunks,
        "slope": chunks,
        "stats": chunks,
        "sums": chunks * (mp_count - 1),
        "far": chunks,
        "onward": chunks * (mp_count - 1),
        "away": chunks * (chips - 1),
        "give": chunks,
        "forward": chunks * (chips - 1),
    }
    names = list(families)

    def kernel(act_ref, cot_ref, gain_ref, up_ref, down_ref, hid_out, grad_out, *refs):
        refs = list(refs)
        take = lambda n: [refs.pop(0) for _ in range(n)]
        up, down, start, gained, relayed = take(5)
        prod_a, prod_b, pair_a, pair_b, cross_a, cross_b = take(6)
        hid, slope, stats, branch, landed, ready = take(6)
        local_sem = take(1)[0]
        sems = {name: take(2) for name in names}

        me, mp_no = lax.axis_index("dp"), lax.axis_index("mp")
        section = lax.axis_index("section")
        chip, core = me // 2, lax.rem(me, 2)
        partner = {"dp": chip * 2 + 1 - core}
        far = {"section": 1 - section}
        ring = [lax.rem(mp_no + step, mp_count) for step in range(mp_count)]
        dp_ring = [lax.rem(me + step, dp_count) for step in range(dp_count)]
        stage_a = (prod_a, pair_a, cross_a, "pair_a", "cross_a")
        stage_b = (prod_b, pair_b, cross_b, "pair_b", "cross_b")
        my_half = pl.ds(pl.multiple_of(core * half, half), half)
        other_half = pl.ds(pl.multiple_of((1 - core) * half, half), half)
        my_rows = pl.ds(pl.multiple_of(me * sub, sub), sub)
        owned = lambda z: pl.ds(pl.multiple_of(z * own, own), own)
        ext = pl.ds(ff, 128)

        def remote(name, at, src, dst, device):
            send, recv = sems[name]
            return pltpu.make_async_remote_copy(
                src_ref=src,
                dst_ref=dst,
                send_sem=send.at[at],
                recv_sem=recv.at[at],
                device_id=device,
                device_id_type=MESH,
            )

        def rows_of(ref, k, column_block):
            return ref.at[
                (k * sub) // row_count,
                pl.ds((k * sub) % row_count, sub),
                pl.ds(pl.multiple_of(column_block * width, width), width),
            ]

        def swap_copy(ref, k, step):
            return remote(
                "swap",
                k * (dp_count - 1) + step - 1,
                rows_of(ref, k, dp_ring[step]),
                start.at[k, my_rows],
                {"dp": dp_ring[step]},
            )

        def swap_own(ref, k):
            return pltpu.make_async_copy(
                rows_of(ref, k, me), start.at[k, my_rows], local_sem.at[2 + k]
            )

        def pair_copy(stage, k):
            prod, pair, _, name, _ = stage
            return remote(name, k, prod.at[k, other_half], pair.at[k], partner)

        def cross_copy(stage, k, hop):
            prod, _, cross, _, name = stage
            bit = lax.rem(chip // (1 << hop), 2)
            other = chip + (1 << hop) * (1 - 2 * bit)
            return remote(
                name,
                k * hops + hop,
                prod.at[k, my_half],
                cross.at[k, hop],
                {"dp": other * 2 + core},
            )

        def half_copy(name, ref, k):
            return remote(name, k, ref.at[k, my_half], ref.at[k, my_half], partner)

        def sum_copy(k, step, columns):
            return remote(
                "sums",
                k * (mp_count - 1) + step - 1,
                branch.at[k, owned(ring[step]), pl.ds(0, columns)],
                landed.at[k, step - 1, :, pl.ds(0, columns)],
                {"mp": ring[step]},
            )

        def far_copy(k):
            return remote("far", k, ready.at[k], relayed.at[k, owned(mp_no)], far)

        def onward_copy(k, step):
            rows_here = relayed.at[k, owned(mp_no)]
            return remote(
                "onward", k * (mp_count - 1) + step - 1, rows_here, rows_here, {"mp": ring[step]}
            )

        def away_copy(slab, k, step):
            other = lax.rem(chip + step, chips)
            return remote(
                "away",
                k * (chips - 1) + step - 1,
                slab.at[k],
                grad_out.at[me, k],
                {"dp": other * 2 + core},
            )

        def give_copy(slab, k):
            return remote("give", k, slab.at[k], grad_out.at[me, k], partner)

        def keep_copy(slab, k):
            return pltpu.make_async_copy(
                slab.at[k], grad_out.at[me, k], local_sem.at[2 + chunks + k]
            )

        def hid_copy(k):
            return pltpu.make_async_copy(hid.at[k], hid_out.at[k], local_sem.at[2 + 2 * chunks + k])

        def forward_copy(k, step):
            source = lax.rem(chip + chips - step, chips)
            block = grad_out.at[source * 2 + core, k]
            return remote("forward", k * (chips - 1) + step - 1, block, block, partner)

        def split(column):
            high = column.astype(low).astype(f32)
            lanes = lax.broadcasted_iota(jnp.int32, (column.shape[0], 128), 1)
            return jnp.where(lanes < 64, high, column - high).astype(low)

        def joined(block):
            wide = block.astype(f32)
            return wide[:, 0:1] + wide[:, 64:65]

        def each_tile(total, tile, body):
            @pl.loop(0, total // tile)
            def _(at):
                body(pl.ds(pl.multiple_of(at * tile, tile), tile))

        gain = gain_ref[:, pl.ds(pl.multiple_of(me * width, width), width)]

        def product(stage, k, source, weight, with_gain):
            prod = stage[0]
            wide = source[k].astype(f32)
            prod[k, :, ext] = split(jnp.sum(wide * wide, axis=1, keepdims=True))
            if with_gain:
                gained[...] = (wide * gain).astype(low)

            def tile(cols):
                left = gained[...] if with_gain else source[k]
                prod[k, :, cols] = matmul(left, weight[:, cols]).astype(low)

            each_tile(ff, ff_tile, tile)
            pair_copy(stage, k).start()

        def add_half(stage, k, other):
            prod = stage[0]

            def tile(cols):
                prod[k, my_half, cols] = (
                    prod[k, my_half, cols].astype(f32) + other[:, cols].astype(f32)
                ).astype(low)

            prod[k, my_half, ext] = split(joined(prod[k, my_half, ext]) + joined(other[:, ext]))
            each_tile(ff, ff_tile, tile)

        def fold(stage, k):
            pair_copy(stage, k).wait_recv()
            add_half(stage, k, stage[1].at[k])
            cross_copy(stage, k, 0).start()

        def crossed(stage, k):
            for hop in range(hops):
                cross_copy(stage, k, hop).wait_recv()
                if hop < hops - 1:
                    cross_copy(stage, k, hop).wait_send()
                    add_half(stage, k, stage[2].at[k, hop])
                    cross_copy(stage, k, hop + 1).start()

        def total_of(stage, k, cols):
            prod, _, cross = stage[:3]
            return prod[k, my_half, cols].astype(f32) + cross[k, hops - 1, :, cols].astype(f32)

        def inverse_rms(stage, k):
            prod, _, cross = stage[:3]
            squares = joined(prod[k, my_half, ext]) + joined(cross[k, hops - 1, :, ext])
            return lax.rsqrt(squares / model + norm_epsilon)

        def activate(k):
            crossed(stage_a, k)
            scale = inverse_rms(stage_a, k)

            def tile(cols):
                pre = total_of(stage_a, k, cols) * scale
                hid[k, my_half, cols] = (pre / (1.0 + jnp.exp(-pre))).astype(low)

            each_tile(ff, ff_tile, tile)
            half_copy("hidden", hid, k).start()

        def multiply_back(k, values, weight):
            def tile(cols):
                branch[k, :, cols] = matmul(values[k], weight[cols, :], 1, 1).astype(low)

            each_tile(width, out_tile, tile)

        def descend(k):
            half_copy("hidden", hid, k).wait_recv()
            hid_copy(k).start()
            multiply_back(k, hid, down)
            for step in range(1, mp_count):
                sum_copy(k, step, width).start()

        def reduced(k, columns):
            for step in range(1, mp_count):
                sum_copy(k, step, columns).wait_recv()
            cols = pl.ds(0, width)
            total = branch[k, owned(mp_no), cols].astype(f32)
            for step in range(1, mp_count):
                total += landed[k, step - 1, :, cols].astype(f32)
            return total

        def finish_forward(k):
            total = reduced(k, width)
            ready[k] = (start[k, owned(mp_no), :].astype(f32) + total).astype(low)
            far_copy(k).start()

        def backward(k):
            crossed(stage_a, k)
            crossed(stage_b, k)
            scale = inverse_rms(stage_b, k)

            def tile(at, dot):
                cols = pl.ds(pl.multiple_of(at * ff_tile, ff_tile), ff_tile)
                summed = total_of(stage_b, k, cols)
                pre = summed * scale
                gate = 1.0 / (1.0 + jnp.exp(-pre))
                hid[k, my_half, cols] = (pre * gate).astype(low)
                grad_pre = (
                    total_of(stage_a, k, cols) * (gate * (1.0 + pre * (1.0 - gate)))
                ).astype(low)
                slope[k, my_half, cols] = grad_pre
                return dot + jnp.sum(summed * grad_pre.astype(f32), axis=1, keepdims=True)

            dot = lax.fori_loop(0, ff // ff_tile, tile, jnp.zeros((half, 1), f32))
            stats[k, my_half, pl.ds(0, 128)] = jnp.broadcast_to(scale, (half, 128))
            stats[k, my_half, pl.ds(128, 128)] = jnp.broadcast_to(dot, (half, 128))
            half_copy("slope", slope, k).start()
            half_copy("stats", stats, k).start()
            half_copy("hidden", hid, k).start()

        def ascend(k):
            half_copy("stats", stats, k).wait_recv()
            branch[k, :, pl.ds(width, 128)] = split(stats[k, :, pl.ds(128, 128)][:, 0:1])
            half_copy("slope", slope, k).wait_recv()
            multiply_back(k, slope, up)
            for step in range(1, mp_count):
                sum_copy(k, step, width + 128).start()

        def finish_backward(k):
            total = reduced(k, width + 128)
            last = pl.ds(width, 128)
            dot = joined(branch[k, owned(mp_no), last])
            for step in range(1, mp_count):
                dot += joined(landed[k, step - 1, :, last])
            scale = stats[k, owned(mp_no), pl.ds(0, 128)][:, 0:1]
            values = relayed[k, owned(mp_no), :].astype(f32)
            ready[k] = (
                start[k, owned(mp_no), :].astype(f32)
                + scale * (gain * total)
                - values * ((scale * scale * scale / model) * dot)
            ).astype(low)
            far_copy(k).start()

        def pass_on(k):
            far_copy(k).wait_recv()
            for step in range(1, mp_count):
                onward_copy(k, step).start()

        def spread(slab, k):
            for step in range(1, chips):
                away_copy(slab, k, step).start()
            give_copy(slab, k).start()
            keep_copy(slab, k).start()

        def hand_over(slab, k):
            for step in range(1, chips):
                away_copy(slab, k, step).wait_recv()
                forward_copy(k, step).start()

        def begin(ref):
            for k in range(chunks):
                for step in range(1, dp_count):
                    swap_copy(ref, k, step).start()
                swap_own(ref, k).start()

        def started(ref, k):
            swap_own(ref, k).wait()
            for step in range(1, dp_count):
                swap_copy(ref, k, step).wait_recv()

        def finish(ref, slab, stages, names_sent, columns):
            for k in range(chunks):
                for step in range(1, dp_count):
                    swap_copy(ref, k, step).wait_send()
                for stage in stages:
                    pair_copy(stage, k).wait_send()
                    cross_copy(stage, k, hops - 1).wait_send()
                for name, buffer in names_sent:
                    half_copy(name, buffer, k).wait_send()
                for step in range(1, mp_count):
                    sum_copy(k, step, columns).wait_send()
                    onward_copy(k, step).wait_send()
                far_copy(k).wait_send()
                hid_copy(k).wait()
                keep_copy(slab, k).wait()
                give_copy(slab, k).wait()
                for step in range(1, chips):
                    away_copy(slab, k, step).wait_send()
                    forward_copy(k, step).wait()

        up_load = pltpu.make_async_copy(up_ref, up, local_sem.at[0])
        down_load = pltpu.make_async_copy(down_ref, down, local_sem.at[1])
        meet(
            [{"dp": dp_ring[step]} for step in range(1, dp_count)]
            + [{"mp": ring[step]} for step in range(1, mp_count)]
            + [far]
        )

        @pl.when(section == 0)
        def _():
            begin(act_ref)
            up_load.start()
            down_load.start()
            for slot in range(chunks + 3):
                if slot < chunks:
                    started(act_ref, slot)
                    if slot == 0:
                        up_load.wait()
                    product(stage_a, slot, start, up, True)
                if 0 <= slot - 1 < chunks:
                    fold(stage_a, slot - 1)
                if 0 <= slot - 2 < chunks:
                    activate(slot - 2)
                    if slot == 2:
                        down_load.wait()
                    descend(slot - 2)
                if 0 <= slot - 3 < chunks:
                    finish_forward(slot - 3)
            for slot in range(chunks + 2):
                if slot < chunks:
                    pass_on(slot)
                if 0 <= slot - 1 < chunks:
                    for step in range(1, mp_count):
                        onward_copy(slot - 1, step).wait_recv()
                    spread(relayed, slot - 1)
                if 0 <= slot - 2 < chunks:
                    hand_over(relayed, slot - 2)
            finish(act_ref, relayed, [stage_a], [("hidden", hid)], width)

        @pl.when(section != 0)
        def _():
            begin(cot_ref)
            down_load.start()
            up_load.start()
            for slot in range(chunks + 1):
                if slot < chunks:
                    started(cot_ref, slot)
                    if slot == 0:
                        down_load.wait()
                    product(stage_a, slot, start, down, False)
                if 0 <= slot - 1 < chunks:
                    fold(stage_a, slot - 1)
            up_load.wait()
            for slot in range(chunks + 3):
                if slot < chunks:
                    pass_on(slot)
                if 0 <= slot - 1 < chunks:
                    for step in range(1, mp_count):
                        onward_copy(slot - 1, step).wait_recv()
                    product(stage_b, slot - 1, relayed, up, True)
                    fold(stage_b, slot - 1)
                if 0 <= slot - 2 < chunks:
                    backward(slot - 2)
                    ascend(slot - 2)
                if 0 <= slot - 3 < chunks:
                    finish_backward(slot - 3)
            for k in range(chunks):
                spread(start, k)
            for k in range(chunks):
                half_copy("hidden", hid, k).wait_recv()
                hid_copy(k).start()
            for k in range(chunks):
                hand_over(start, k)
            finish(
                cot_ref,
                start,
                [stage_a, stage_b],
                [("hidden", hid), ("slope", slope), ("stats", stats)],
                width + 128,
            )

    dma = pltpu.SemaphoreType.DMA
    vmem = pltpu.VMEM
    scratch = [
        vmem((width, ff), low),
        vmem((width, ff), low),
        vmem((chunks, tall, width), low),
        vmem((tall, width), low),
        vmem((chunks, tall, width), low),
        vmem((chunks, tall, ff + 128), low),
        vmem((chunks, tall, ff + 128), low),
        vmem((chunks, half, ff + 128), low),
        vmem((chunks, half, ff + 128), low),
        vmem((chunks, hops, half, ff + 128), low),
        vmem((chunks, hops, half, ff + 128), low),
        vmem((chunks, tall, ff), low),
        vmem((chunks, tall, ff), low),
        vmem((chunks, tall, 256), f32),
        vmem((chunks, tall, width + 128), low),
        vmem((chunks, mp_count - 1, own, width + 128), low),
        vmem((chunks, own, width), low),
        dma((2 + 3 * chunks,)),
    ]
    for name in names:
        scratch += [dma((families[name],)), dma((families[name],))]
    return pl.pallas_call(
        kernel,
        out_shape=[
            jax.ShapeDtypeStruct((chunks, tall, ff), low),
            jax.ShapeDtypeStruct((dp_count, chunks, tall, width), low),
        ],
        in_specs=[
            pl.BlockSpec(memory_space=pl.ANY),
            pl.BlockSpec(memory_space=pl.ANY),
            pl.BlockSpec(memory_space=pltpu.VMEM),
            pl.BlockSpec(memory_space=pl.ANY),
            pl.BlockSpec(memory_space=pl.ANY),
        ],
        out_specs=[pl.BlockSpec(memory_space=pl.ANY)] * 2,
        scratch_shapes=scratch,
        compiler_params=pltpu.CompilerParams(
            collective_id=0, has_side_effects=True, vmem_limit_bytes=VMEM_LIMIT
        ),
        name="relay",
    )(activations, cotangent, gain_rows, w_up, w_down)


def inverse_root(matrix):
    low = jnp.bfloat16
    order = matrix.shape[-1]
    on_diagonal = lax.broadcasted_iota(jnp.int32, (order, order), 0) == lax.broadcasted_iota(
        jnp.int32, (order, order), 1
    )
    identity = jnp.where(on_diagonal, 1.0, 0.0).astype(jnp.float32)
    shifted = matrix + ridge_shift * identity
    norm_sq = jnp.sum(jnp.sum(shifted * shifted, axis=1, keepdims=True), axis=0, keepdims=True)
    factor = 2.5 / jnp.sqrt(norm_sq)
    moment = factor * shifted
    moment_low = moment.astype(low)
    moment_sq = matmul(moment_low, moment_low)
    square = (1.5625 * identity - 0.625 * moment + 0.0625 * moment_sq).astype(low)
    stepped = (1.25 * moment - 0.25 * moment_sq).astype(low)
    third = matmul(square, stepped).astype(low)
    fifth = matmul(square, third)
    scale = jnp.sqrt(jnp.sqrt(factor))
    return scale * (1.5625 * identity - 0.3125 * moment - 0.25 * fifth)


def precondition(block_row, block_col, due, hidden, grads, gram_l, gram_r, root_l, root_r):
    slots = gram_l.shape[0]
    tokens = hidden.shape[0]
    width = grads.shape[2]
    scale = 1.0 / math.sqrt(tokens)

    def kernel(
        row_ref, col_ref, due_ref, hid_ref, grad_ref, gl_ref, gr_ref, rl_ref, rr_ref,
        gl_out, gr_out, rl_out, rr_out, up_out,
    ):
        slot = pl.program_id(0)
        pieces = [grad_ref[piece] for piece in range(grad_ref.shape[0])]
        dy = pieces[0] if len(pieces) == 1 else jnp.concatenate(pieces, axis=1)
        grad_low = (matmul(hid_ref[...], dy, 0, 0) * scale).astype(jnp.bfloat16)
        gl_out[0] = decay_rate * gl_ref[0] + matmul(grad_low, grad_low, 1, 1) * (1.0 / BLK)
        gr_out[0] = decay_rate * gr_ref[0] + matmul(grad_low, grad_low, 0, 0) * (1.0 / BLK)

        @pl.when(due_ref[slot] != 0)
        def _():
            rl_out[0] = inverse_root(gl_out[0]).astype(jnp.bfloat16)
            rr_out[0] = inverse_root(gr_out[0]).astype(jnp.bfloat16)

        @pl.when(due_ref[slot] == 0)
        def _():
            rl_out[0] = rl_ref[0]
            rr_out[0] = rr_ref[0]

        right_part = matmul(grad_low, rr_out[0]).astype(jnp.bfloat16)
        up_out[0] = matmul(rl_out[0], right_part).astype(jnp.bfloat16)

    if width >= BLK:
        per = width // BLK
        grad_spec = pl.BlockSpec(
            (1, tokens, BLK),
            lambda s, row, col, due: (lax.div(col[s], per), 0, lax.rem(col[s], per)),
        )
    else:
        grad_spec = pl.BlockSpec(
            (BLK // width, tokens, width), lambda s, row, col, due: (col[s], 0, 0)
        )
    square_spec = pl.BlockSpec((1, BLK, BLK), lambda s, row, col, due: (s, 0, 0))
    return pl.pallas_call(
        kernel,
        grid_spec=pltpu.PrefetchScalarGridSpec(
            num_scalar_prefetch=3,
            grid=(slots,),
            in_specs=[
                pl.BlockSpec((tokens, BLK), lambda s, row, col, due: (0, row[s])),
                grad_spec,
            ]
            + [square_spec] * 4,
            out_specs=[square_spec] * 5,
        ),
        out_shape=[
            jax.ShapeDtypeStruct(gram_l.shape, jnp.float32),
            jax.ShapeDtypeStruct(gram_l.shape, jnp.float32),
            jax.ShapeDtypeStruct(gram_l.shape, jnp.bfloat16),
            jax.ShapeDtypeStruct(gram_l.shape, jnp.bfloat16),
            jax.ShapeDtypeStruct(gram_l.shape, jnp.bfloat16),
        ],
        compiler_params=pltpu.CompilerParams(
            dimension_semantics=("arbitrary",), vmem_limit_bytes=VMEM_LIMIT
        ),
    )(block_row, block_col, due, hidden, grads, gram_l, gram_r, root_l, root_r)


def on_device(
    activations,
    cotangent,
    norm_gain,
    w_up,
    w_down,
    gram_left,
    gram_right,
    root_left,
    root_right,
    owner_slot,
    eighth,
    refresh_phase,
):
    section_no = lax.axis_index("section")
    dp_no = lax.axis_index("dp")
    mp_no = lax.axis_index("mp")
    dp_count = lax.axis_size("dp")
    mp_count = lax.axis_size("mp")
    micro_count, row_count, model_width = activations.shape
    rows = micro_count * row_count
    tokens = rows * dp_count
    width, shard_ff = w_up.shape[1:]

    block_cols = model_width // BLK
    block_rows = shard_ff // BLK
    group = block_rows * block_cols
    per_dev = gram_left.shape[1]
    pick = lambda table: lax.dynamic_slice_in_dim(
        lax.dynamic_index_in_dim(table, section_no, 0, keepdims=False), mp_no * block_rows, block_rows, 0
    ).reshape(-1)
    slots = (dp_no * mp_count + mp_no) * per_dev + jnp.arange(per_dev, dtype=jnp.int32)
    owned = pick(owner_slot)[None, :] == slots[:, None]
    block = jnp.sum(jnp.where(owned, jnp.arange(group, dtype=jnp.int32)[None, :], 0), axis=1)
    is_due = pick(eighth) == refresh_phase[0] % 8
    due = jnp.sum(jnp.where(owned & is_due[None, :], 1, 0), axis=1).astype(jnp.int32)

    hidden, grads = relay(activations, cotangent, norm_gain, w_up[0], w_down[0])

    results = precondition(
        block // block_cols,
        block % block_cols,
        due,
        hidden.reshape(tokens, shard_ff),
        grads.reshape(dp_count, tokens, width),
        gram_left[0],
        gram_right[0],
        root_left[0],
        root_right[0],
    )
    return tuple(result[None] for result in results)


def solution(mesh):
    return jax.shard_map(
        on_device,
        mesh=mesh,
        in_specs=(
            P(None, "dp", None),
            P(None, "dp", None),
            P("section", None),
            P("section", "dp", "mp"),
            P("section", "dp", "mp"),
            P("section", ("dp", "mp"), None, None),
            P("section", ("dp", "mp"), None, None),
            P("section", ("dp", "mp"), None, None),
            P("section", ("dp", "mp"), None, None),
            P(),
            P(),
            P(),
        ),
        out_specs=(
            P("section", ("dp", "mp"), None, None),
            P("section", ("dp", "mp"), None, None),
            P("section", ("dp", "mp"), None, None),
            P("section", ("dp", "mp"), None, None),
            P("section", ("dp", "mp"), None, None),
        ),
        check_vma=False,
    )
```

```python
import math

import jax
import jax.numpy as jnp
from jax import lax
from jax.experimental import pallas as pl
from jax.experimental.pallas import tpu as pltpu
from jax.sharding import PartitionSpec as P

BLK = 512
MESH = pl.DeviceIdType.MESH
VMEM_LIMIT = 60 * 1024 * 1024

norm_epsilon = 1e-05
decay_rate = 0.9
ridge_shift = 0.001


def meet(devices):
    barrier = pltpu.get_barrier_semaphore()
    for device in devices:
        pl.semaphore_signal(barrier, inc=1, device_id=device, device_id_type=MESH)
    pl.semaphore_wait(barrier, len(devices))


def chunks_of(rows, row_count):
    fits = lambda n: rows % n == 0 and row_count % (rows // n) == 0 and (rows // n) % 16 == 0
    return max([n for n in (1, 2, 4) if fits(n)])


def matmul(left, right, left_dim=1, right_dim=0):
    return lax.dot_general(
        left, right, (((left_dim,), (right_dim,)), ((), ())), preferred_element_type=jnp.float32
    )


def relay(activations, cotangent, gain_rows, w_up, w_down):
    micro_count, row_count, model = activations.shape
    width, ff = w_up.shape
    dp_count, mp_count = lax.axis_size("dp"), lax.axis_size("mp")
    chips = dp_count // 2
    hops = chips.bit_length() - 1
    rows = micro_count * row_count
    chunks = chunks_of(rows, row_count)
    sub = rows // chunks
    tall = sub * dp_count
    half, own = tall // 2, tall // mp_count
    ff_tile, out_tile = min(512, ff), min(256, width)
    low, f32 = jnp.bfloat16, jnp.float32

    families = {
        "swap": chunks * (dp_count - 1),
        "pair_a": chunks,
        "pair_b": chunks,
        "cross_a": chunks * hops,
        "cross_b": chunks * hops,
        "hidden": chunks,
        "slope": chunks,
        "stats": chunks,
        "sums": chunks * (mp_count - 1),
        "far": chunks,
        "onward": chunks * (mp_count - 1),
        "away": chunks * mp_count * (chips - 1),
        "give": chunks * mp_count,
        "forward": chunks * mp_count * (chips - 1),
    }
    names = list(families)

    def kernel(act_ref, cot_ref, gain_ref, up_ref, down_ref, hid_out, grad_out, *refs):
        refs = list(refs)
        take = lambda n: [refs.pop(0) for _ in range(n)]
        up, down, start, gained, relayed = take(5)
        prod_a, prod_b, pair_a, pair_b, cross_a, cross_b = take(6)
        hid, slope, stats, branch, landed, ready = take(6)
        local_sem = take(1)[0]
        sems = {name: take(2) for name in names}

        me, mp_no = lax.axis_index("dp"), lax.axis_index("mp")
        section = lax.axis_index("section")
        chip, core = me // 2, lax.rem(me, 2)
        partner = {"dp": chip * 2 + 1 - core}
        ring = [lax.rem(mp_no + step, mp_count) for step in range(mp_count)]
        origin = [lax.rem(mp_no + mp_count - step, mp_count) for step in range(mp_count)]
        far = {"section": 1 - section}
        dp_ring = [lax.rem(me + step, dp_count) for step in range(dp_count)]
        stage_a = (prod_a, pair_a, cross_a, "pair_a", "cross_a")
        stage_b = (prod_b, pair_b, cross_b, "pair_b", "cross_b")
        my_half = pl.ds(pl.multiple_of(core * half, half), half)
        other_half = pl.ds(pl.multiple_of((1 - core) * half, half), half)
        my_rows = pl.ds(pl.multiple_of(me * sub, sub), sub)
        owned = lambda z: pl.ds(pl.multiple_of(z * own, own), own)
        ext = pl.ds(ff, 128)

        def remote(name, at, src, dst, device):
            send, recv = sems[name]
            return pltpu.make_async_remote_copy(
                src_ref=src,
                dst_ref=dst,
                send_sem=send.at[at],
                recv_sem=recv.at[at],
                device_id=device,
                device_id_type=MESH,
            )

        def rows_of(ref, k, column_block):
            return ref.at[
                (k * sub) // row_count,
                pl.ds((k * sub) % row_count, sub),
                pl.ds(pl.multiple_of(column_block * width, width), width),
            ]

        def swap_copy(ref, k, step):
            return remote(
                "swap",
                k * (dp_count - 1) + step - 1,
                rows_of(ref, k, dp_ring[step]),
                start.at[k, my_rows],
                {"dp": dp_ring[step]},
            )

        def swap_own(ref, k):
            return pltpu.make_async_copy(
                rows_of(ref, k, me), start.at[k, my_rows], local_sem.at[2 + k]
            )

        def pair_copy(stage, k):
            prod, pair, _, name, _ = stage
            return remote(name, k, prod.at[k, other_half], pair.at[k], partner)

        def cross_copy(stage, k, hop):
            prod, _, cross, _, name = stage
            bit = lax.rem(chip // (1 << hop), 2)
            other = chip + (1 << hop) * (1 - 2 * bit)
            return remote(
                name,
                k * hops + hop,
                prod.at[k, my_half],
                cross.at[k, hop],
                {"dp": other * 2 + core},
            )

        def half_copy(name, ref, k):
            return remote(name, k, ref.at[k, my_half], ref.at[k, my_half], partner)

        def sum_copy(k, step, columns):
            return remote(
                "sums",
                k * (mp_count - 1) + step - 1,
                branch.at[k, owned(ring[step]), pl.ds(0, columns)],
                landed.at[k, step - 1, :, pl.ds(0, columns)],
                {"mp": ring[step]},
            )

        def far_copy(k):
            return remote("far", k, ready.at[k], relayed.at[k, owned(mp_no)], far)

        def onward_copy(k, step):
            rows_here = relayed.at[k, owned(mp_no)]
            return remote(
                "onward", k * (mp_count - 1) + step - 1, rows_here, rows_here, {"mp": ring[step]}
            )

        def away_copy(slab, k, piece, step):
            other = lax.rem(chip + step, chips)
            rows_here = owned(origin[piece])
            return remote(
                "away",
                (k * mp_count + piece) * (chips - 1) + step - 1,
                slab.at[k, rows_here],
                grad_out.at[me, k, rows_here],
                {"dp": other * 2 + core},
            )

        def give_copy(slab, k, piece):
            rows_here = owned(origin[piece])
            return remote(
                "give",
                k * mp_count + piece,
                slab.at[k, rows_here],
                grad_out.at[me, k, rows_here],
                partner,
            )

        def keep_copy(slab, k):
            return pltpu.make_async_copy(
                slab.at[k], grad_out.at[me, k], local_sem.at[2 + chunks + k]
            )

        def hid_copy(k):
            return pltpu.make_async_copy(hid.at[k], hid_out.at[k], local_sem.at[2 + 2 * chunks + k])

        def forward_copy(k, piece, step):
            source = lax.rem(chip + chips - step, chips)
            block = grad_out.at[source * 2 + core, k, owned(origin[piece])]
            return remote(
                "forward", (k * mp_count + piece) * (chips - 1) + step - 1, block, block, partner
            )

        def split(column):
            high = column.astype(low).astype(f32)
            lanes = lax.broadcasted_iota(jnp.int32, (column.shape[0], 128), 1)
            return jnp.where(lanes < 64, high, column - high).astype(low)

        def joined(block):
            wide = block.astype(f32)
            return wide[:, 0:1] + wide[:, 64:65]

        def each_tile(total, tile, body):
            @pl.loop(0, total // tile)
            def _(at):
                body(pl.ds(pl.multiple_of(at * tile, tile), tile))

        gain = gain_ref[:, pl.ds(pl.multiple_of(me * width, width), width)]

        def product(stage, k, source, weight, with_gain):
            prod = stage[0]
            wide = source[k].astype(f32)
            prod[k, :, ext] = split(jnp.sum(wide * wide, axis=1, keepdims=True))
            if with_gain:
                gained[...] = (wide * gain).astype(low)

            def tile(cols):
                left = gained[...] if with_gain else source[k]
                prod[k, :, cols] = matmul(left, weight[:, cols]).astype(low)

            each_tile(ff, ff_tile, tile)
            pair_copy(stage, k).start()

        def add_half(stage, k, other):
            prod = stage[0]

            def tile(cols):
                prod[k, my_half, cols] = (
                    prod[k, my_half, cols].astype(f32) + other[:, cols].astype(f32)
                ).astype(low)

            prod[k, my_half, ext] = split(joined(prod[k, my_half, ext]) + joined(other[:, ext]))
            each_tile(ff, ff_tile, tile)

        def fold(stage, k):
            pair_copy(stage, k).wait_recv()
            add_half(stage, k, stage[1].at[k])
            cross_copy(stage, k, 0).start()

        def crossed(stage, k):
            for hop in range(hops):
                cross_copy(stage, k, hop).wait_recv()
                if hop < hops - 1:
                    cross_copy(stage, k, hop).wait_send()
                    add_half(stage, k, stage[2].at[k, hop])
                    cross_copy(stage, k, hop + 1).start()

        def total_of(stage, k, cols):
            prod, _, cross = stage[:3]
            return prod[k, my_half, cols].astype(f32) + cross[k, hops - 1, :, cols].astype(f32)

        def inverse_rms(stage, k):
            prod, _, cross = stage[:3]
            squares = joined(prod[k, my_half, ext]) + joined(cross[k, hops - 1, :, ext])
            return lax.rsqrt(squares / model + norm_epsilon)

        def activate(k):
            crossed(stage_a, k)
            scale = inverse_rms(stage_a, k)

            def tile(cols):
                pre = total_of(stage_a, k, cols) * scale
                hid[k, my_half, cols] = (pre / (1.0 + jnp.exp(-pre))).astype(low)

            each_tile(ff, ff_tile, tile)
            half_copy("hidden", hid, k).start()

        def multiply_back(k, values, weight):
            def tile(cols):
                branch[k, :, cols] = matmul(values[k], weight[cols, :], 1, 1).astype(low)

            each_tile(width, out_tile, tile)

        def descend(k):
            half_copy("hidden", hid, k).wait_recv()
            hid_copy(k).start()
            multiply_back(k, hid, down)
            for step in range(1, mp_count):
                sum_copy(k, step, width).start()

        def reduced(k, columns):
            for step in range(1, mp_count):
                sum_copy(k, step, columns).wait_recv()
            cols = pl.ds(0, width)
            total = branch[k, owned(mp_no), cols].astype(f32)
            for step in range(1, mp_count):
                total += landed[k, step - 1, :, cols].astype(f32)
            return total

        def finish_forward(k):
            total = reduced(k, width)
            ready[k] = (start[k, owned(mp_no), :].astype(f32) + total).astype(low)
            far_copy(k).start()

        def backward(k):
            crossed(stage_a, k)
            crossed(stage_b, k)
            scale = inverse_rms(stage_b, k)

            def tile(at, dot):
                cols = pl.ds(pl.multiple_of(at * ff_tile, ff_tile), ff_tile)
                summed = total_of(stage_b, k, cols)
                pre = summed * scale
                gate = 1.0 / (1.0 + jnp.exp(-pre))
                hid[k, my_half, cols] = (pre * gate).astype(low)
                grad_pre = (
                    total_of(stage_a, k, cols) * (gate * (1.0 + pre * (1.0 - gate)))
                ).astype(low)
                slope[k, my_half, cols] = grad_pre
                return dot + jnp.sum(summed * grad_pre.astype(f32), axis=1, keepdims=True)

            dot = lax.fori_loop(0, ff // ff_tile, tile, jnp.zeros((half, 1), f32))
            stats[k, my_half, pl.ds(0, 128)] = jnp.broadcast_to(scale, (half, 128))
            stats[k, my_half, pl.ds(128, 128)] = jnp.broadcast_to(dot, (half, 128))
            half_copy("slope", slope, k).start()
            half_copy("stats", stats, k).start()

        def ascend(k):
            half_copy("stats", stats, k).wait_recv()
            branch[k, :, pl.ds(width, 128)] = split(stats[k, :, pl.ds(128, 128)][:, 0:1])
            half_copy("slope", slope, k).wait_recv()
            multiply_back(k, slope, up)
            for step in range(1, mp_count):
                sum_copy(k, step, width + 128).start()
            half_copy("hidden", hid, k).start()

        def finish_backward(k):
            total = reduced(k, width + 128)
            last = pl.ds(width, 128)
            dot = joined(branch[k, owned(mp_no), last])
            for step in range(1, mp_count):
                dot += joined(landed[k, step - 1, :, last])
            scale = stats[k, owned(mp_no), pl.ds(0, 128)][:, 0:1]
            values = relayed[k, owned(mp_no), :].astype(f32)
            ready[k] = (
                start[k, owned(mp_no), :].astype(f32)
                + scale * (gain * total)
                - values * ((scale * scale * scale / model) * dot)
            ).astype(low)
            far_copy(k).start()

        def pass_on(k):
            far_copy(k).wait_recv()
            for step in range(1, mp_count):
                onward_copy(k, step).start()

        def arrived(k):
            for step in range(1, mp_count):
                onward_copy(k, step).wait_recv()

        def spread(slab, k, piece):
            for step in range(1, chips):
                away_copy(slab, k, piece, step).start()
            give_copy(slab, k, piece).start()

        def hand_over(slab, k):
            for piece in range(mp_count):
                for step in range(1, chips):
                    away_copy(slab, k, piece, step).wait_recv()
                    forward_copy(k, piece, step).start()

        def begin(ref):
            for k in range(chunks):
                for step in range(1, dp_count):
                    swap_copy(ref, k, step).start()
                swap_own(ref, k).start()

        def started(ref, k):
            swap_own(ref, k).wait()
            for step in range(1, dp_count):
                swap_copy(ref, k, step).wait_recv()

        def finish(ref, slab, stages, names_sent, columns):
            for k in range(chunks):
                for step in range(1, dp_count):
                    swap_copy(ref, k, step).wait_send()
                for stage in stages:
                    pair_copy(stage, k).wait_send()
                    cross_copy(stage, k, hops - 1).wait_send()
                for name, buffer in names_sent:
                    half_copy(name, buffer, k).wait_send()
                for step in range(1, mp_count):
                    sum_copy(k, step, columns).wait_send()
                    onward_copy(k, step).wait_send()
                far_copy(k).wait_send()
                hid_copy(k).wait()
                keep_copy(slab, k).wait()
                for piece in range(mp_count):
                    give_copy(slab, k, piece).wait()
                    for step in range(1, chips):
                        away_copy(slab, k, piece, step).wait_send()
                        forward_copy(k, piece, step).wait()

        up_load = pltpu.make_async_copy(up_ref, up, local_sem.at[0])
        down_load = pltpu.make_async_copy(down_ref, down, local_sem.at[1])
        meet(
            [{"dp": dp_ring[step]} for step in range(1, dp_count)]
            + [{"mp": ring[step]} for step in range(1, mp_count)]
            + [far]
        )

        @pl.when(section == 0)
        def _():
            begin(act_ref)
            up_load.start()
            down_load.start()
            for slot in range(chunks + 1):
                if slot < chunks:
                    started(act_ref, slot)
                    if slot == 0:
                        up_load.wait()
                    product(stage_a, slot, start, up, True)
                if slot >= 1:
                    fold(stage_a, slot - 1)
            down_load.wait()
            for slot in range(chunks + 1):
                if slot < chunks:
                    activate(slot)
                    descend(slot)
                if slot >= 1:
                    finish_forward(slot - 1)
            for slot in range(chunks + 2):
                if slot < chunks:
                    pass_on(slot)
                    spread(relayed, slot, 0)
                if 0 <= slot - 1 < chunks:
                    for step in range(1, mp_count):
                        onward_copy(slot - 1, step).wait_recv()
                        spread(relayed, slot - 1, step)
                    keep_copy(relayed, slot - 1).start()
                if slot >= 2:
                    hand_over(relayed, slot - 2)
            finish(act_ref, relayed, [stage_a], [("hidden", hid)], width)

        @pl.when(section != 0)
        def _():
            begin(cot_ref)
            down_load.start()
            up_load.start()
            for slot in range(chunks + 1):
                if slot < chunks:
                    started(cot_ref, slot)
                    if slot == 0:
                        down_load.wait()
                    product(stage_a, slot, start, down, False)
                if 0 <= slot - 1 < chunks:
                    fold(stage_a, slot - 1)
            up_load.wait()
            pass_on(0)
            for slot in range(chunks + 3):
                if slot + 1 < chunks:
                    pass_on(slot + 1)
                if slot < chunks:
                    arrived(slot)
                    product(stage_b, slot, relayed, up, True)
                if 0 <= slot - 2 < chunks:
                    ascend(slot - 2)
                if slot < chunks:
                    fold(stage_b, slot)
                if 0 <= slot - 3 < chunks:
                    finish_backward(slot - 3)
                if 0 <= slot - 1 < chunks:
                    backward(slot - 1)
                if slot == chunks:
                    for k in range(chunks):
                        for piece in range(mp_count):
                            spread(start, k, piece)
                        keep_copy(start, k).start()
            for k in range(chunks):
                half_copy("hidden", hid, k).wait_recv()
                hid_copy(k).start()
            for k in range(chunks):
                hand_over(start, k)
            finish(
                cot_ref,
                start,
                [stage_a, stage_b],
                [("hidden", hid), ("slope", slope), ("stats", stats)],
                width + 128,
            )

    dma = pltpu.SemaphoreType.DMA
    vmem = pltpu.VMEM
    scratch = [
        vmem((width, ff), low),
        vmem((width, ff), low),
        vmem((chunks, tall, width), low),
        vmem((tall, width), low),
        vmem((chunks, tall, width), low),
        vmem((chunks, tall, ff + 128), low),
        vmem((chunks, tall, ff + 128), low),
        vmem((chunks, half, ff + 128), low),
        vmem((chunks, half, ff + 128), low),
        vmem((chunks, hops, half, ff + 128), low),
        vmem((chunks, hops, half, ff + 128), low),
        vmem((chunks, tall, ff), low),
        vmem((chunks, tall, ff), low),
        vmem((chunks, tall, 256), f32),
        vmem((chunks, tall, width + 128), low),
        vmem((chunks, mp_count - 1, own, width + 128), low),
        vmem((chunks, own, width), low),
        dma((2 + 3 * chunks,)),
    ]
    for name in names:
        scratch += [dma((families[name],)), dma((families[name],))]
    return pl.pallas_call(
        kernel,
        out_shape=[
            jax.ShapeDtypeStruct((chunks, tall, ff), low),
            jax.ShapeDtypeStruct((dp_count, chunks, tall, width), low),
        ],
        in_specs=[
            pl.BlockSpec(memory_space=pltpu.HBM),
            pl.BlockSpec(memory_space=pltpu.HBM),
            pl.BlockSpec(memory_space=pltpu.VMEM),
            pl.BlockSpec(memory_space=pltpu.HBM),
            pl.BlockSpec(memory_space=pltpu.HBM),
        ],
        out_specs=[pl.BlockSpec(memory_space=pl.ANY)] * 2,
        scratch_shapes=scratch,
        compiler_params=pltpu.CompilerParams(
            collective_id=0, has_side_effects=True, vmem_limit_bytes=VMEM_LIMIT
        ),
        name="relay",
    )(activations, cotangent, gain_rows, w_up, w_down)


def inverse_root(matrix):
    low = jnp.bfloat16
    order = matrix.shape[-1]
    on_diagonal = lax.broadcasted_iota(jnp.int32, (order, order), 0) == lax.broadcasted_iota(
        jnp.int32, (order, order), 1
    )
    identity = jnp.where(on_diagonal, 1.0, 0.0).astype(jnp.float32)
    shifted = matrix + ridge_shift * identity
    norm_sq = jnp.sum(jnp.sum(shifted * shifted, axis=1, keepdims=True), axis=0, keepdims=True)
    factor = 2.5 / jnp.sqrt(norm_sq)
    moment = factor * shifted
    moment_low = moment.astype(low)
    moment_sq = matmul(moment_low, moment_low)
    square = (1.5625 * identity - 0.625 * moment + 0.0625 * moment_sq).astype(low)
    stepped = (1.25 * moment - 0.25 * moment_sq).astype(low)
    third = matmul(square, stepped).astype(low)
    fifth = matmul(square, third)
    scale = jnp.sqrt(jnp.sqrt(factor))
    return scale * (1.5625 * identity - 0.3125 * moment - 0.25 * fifth)


def precondition(hidden, grads, grams_and_roots, owner_slot, eighth, refresh_phase, block_cols):
    slots = grams_and_roots[0].shape[0]
    tokens, shard_ff = hidden.shape
    width = grads.shape[2]
    block_rows = shard_ff // BLK
    scale = 1.0 / math.sqrt(tokens)
    pieces = max(BLK // width, 1)
    per = max(width // BLK, 1)

    def kernel(
        owner_ref, eighth_ref, phase_ref, hid_ref, grad_ref, gl_ref, gr_ref, rl_ref, rr_ref,
        gl_out, gr_out, rl_out, rr_out, up_out,
        hid, dy, gl, gr, rl, rr, block, due, sem,
    ):
        slot = pl.program_id(0)

        def loads(at):
            row, col = lax.div(block[at], block_cols), lax.rem(block[at], block_cols)
            copy = lambda src, dst, n: pltpu.make_async_copy(src, dst, sem.at[at, n])
            copies = [
                copy(hid_ref.at[:, pl.ds(pl.multiple_of(row * BLK, BLK), BLK)], hid.at[at], 0)
            ]
            if width >= BLK:
                first = pl.multiple_of(lax.rem(col, per) * BLK, BLK)
                source = grad_ref.at[lax.div(col, per), :, pl.ds(first, BLK)]
                copies.append(copy(source, dy.at[at], 1))
            else:
                for piece in range(pieces):
                    target = dy.at[at, :, pl.ds(piece * width, width)]
                    copies.append(copy(grad_ref.at[col * pieces + piece], target, 1 + piece))
            sources = ((gl_ref, gl), (gr_ref, gr), (rl_ref, rl), (rr_ref, rr))
            for n, (source, target) in enumerate(sources):
                copies.append(copy(source.at[at], target.at[at], 1 + pieces + n))
            return copies

        @pl.when(slot == 0)
        def _():
            section, mp_no = lax.axis_index("section"), lax.axis_index("mp")
            base = (lax.axis_index("dp") * lax.axis_size("mp") + mp_no) * slots
            phase = lax.rem(phase_ref[0], 8)

            @pl.loop(0, block_rows * block_cols)
            def _(at):
                row, col = mp_no * block_rows + lax.div(at, block_cols), lax.rem(at, block_cols)
                place = owner_ref[section, col, row] - base

                @pl.when((place >= 0) & (place < slots))
                def _():
                    block[place] = at
                    due[place] = jnp.where(eighth_ref[section, col, row] == phase, 1, 0)

            @pl.loop(0, slots)
            def _(at):
                for copy in loads(at):
                    copy.start()

        copies = loads(slot)
        for copy in copies[: 1 + pieces]:
            copy.wait()
        grad_low = (matmul(hid[slot], dy[slot], 0, 0) * scale).astype(jnp.bfloat16)
        for copy in copies[1 + pieces :]:
            copy.wait()
        gl_out[0] = decay_rate * gl[slot] + matmul(grad_low, grad_low, 1, 1) * (1.0 / BLK)
        gr_out[0] = decay_rate * gr[slot] + matmul(grad_low, grad_low, 0, 0) * (1.0 / BLK)

        @pl.when(due[slot] != 0)
        def _():
            rl_out[0] = inverse_root(gl_out[0]).astype(jnp.bfloat16)
            rr_out[0] = inverse_root(gr_out[0]).astype(jnp.bfloat16)

        @pl.when(due[slot] == 0)
        def _():
            rl_out[0] = rl[slot]
            rr_out[0] = rr[slot]

        right_part = matmul(grad_low, rr_out[0]).astype(jnp.bfloat16)
        up_out[0] = matmul(rl_out[0], right_part).astype(jnp.bfloat16)

    low, f32 = jnp.bfloat16, jnp.float32
    square_spec = pl.BlockSpec((1, BLK, BLK), lambda s: (s, 0, 0))
    square = lambda dtype: jax.ShapeDtypeStruct((slots, BLK, BLK), dtype)
    return pl.pallas_call(
        kernel,
        grid=(slots,),
        in_specs=[pl.BlockSpec(memory_space=pltpu.SMEM)] * 3
        + [pl.BlockSpec(memory_space=pl.ANY)] * 6,
        out_specs=[square_spec] * 5,
        out_shape=[square(f32), square(f32), square(low), square(low), square(low)],
        scratch_shapes=[
            pltpu.VMEM((slots, tokens, BLK), low),
            pltpu.VMEM((slots, tokens, BLK), low),
            pltpu.VMEM((slots, BLK, BLK), f32),
            pltpu.VMEM((slots, BLK, BLK), f32),
            pltpu.VMEM((slots, BLK, BLK), low),
            pltpu.VMEM((slots, BLK, BLK), low),
            pltpu.SMEM((slots,), jnp.int32),
            pltpu.SMEM((slots,), jnp.int32),
            pltpu.SemaphoreType.DMA((slots, 5 + pieces)),
        ],
        compiler_params=pltpu.CompilerParams(
            dimension_semantics=("arbitrary",), vmem_limit_bytes=VMEM_LIMIT
        ),
        name="precondition",
    )(owner_slot, eighth, refresh_phase, hidden, grads, *grams_and_roots)


def on_device(
    activations,
    cotangent,
    norm_gain,
    w_up,
    w_down,
    gram_left,
    gram_right,
    root_left,
    root_right,
    owner_slot,
    eighth,
    refresh_phase,
):
    width, shard_ff = w_up.shape[1:]
    hidden, grads = relay(activations, cotangent, norm_gain, w_up[0], w_down[0])
    results = precondition(
        hidden.reshape(-1, shard_ff),
        grads.reshape(grads.shape[0], -1, width),
        [x[0] for x in (gram_left, gram_right, root_left, root_right)],
        owner_slot.swapaxes(1, 2),
        eighth.swapaxes(1, 2),
        refresh_phase,
        activations.shape[2] // BLK,
    )
    return tuple(result[None] for result in results)


def solution(mesh):
    return jax.shard_map(
        on_device,
        mesh=mesh,
        in_specs=(
            P(None, "dp", None),
            P(None, "dp", None),
            P("section", None),
            P("section", "dp", "mp"),
            P("section", "dp", "mp"),
            P("section", ("dp", "mp"), None, None),
            P("section", ("dp", "mp"), None, None),
            P("section", ("dp", "mp"), None, None),
            P("section", ("dp", "mp"), None, None),
            P(),
            P(),
            P(),
        ),
        out_specs=(
            P("section", ("dp", "mp"), None, None),
            P("section", ("dp", "mp"), None, None),
            P("section", ("dp", "mp"), None, None),
            P("section", ("dp", "mp"), None, None),
            P("section", ("dp", "mp"), None, None),
        ),
        check_vma=False,
    )
```

```python
import math

import jax
import jax.numpy as jnp
from jax import lax
from jax.experimental import pallas as pl
from jax.experimental.pallas import tpu as pltpu
from jax.sharding import PartitionSpec as P

BLK = 512
MESH = pl.DeviceIdType.MESH
VMEM_LIMIT = 60 * 1024 * 1024

norm_epsilon = 1e-05
decay_rate = 0.9
ridge_shift = 0.001


def meet(devices):
    barrier = pltpu.get_barrier_semaphore()
    for device in devices:
        pl.semaphore_signal(barrier, inc=1, device_id=device, device_id_type=MESH)
    pl.semaphore_wait(barrier, len(devices))


def chunks_of(rows, row_count):
    fits = lambda n: rows % n == 0 and row_count % (rows // n) == 0 and (rows // n) % 16 == 0
    return max([n for n in (1, 2, 4) if fits(n)])


def matmul(left, right, left_dim=1, right_dim=0):
    return lax.dot_general(
        left, right, (((left_dim,), (right_dim,)), ((), ())), preferred_element_type=jnp.float32
    )


def relay(activations, cotangent, gain_rows, w_up, w_down):
    micro_count, row_count, model = activations.shape
    width, ff = w_up.shape
    dp_count, mp_count = lax.axis_size("dp"), lax.axis_size("mp")
    chips = dp_count // 2
    hops = chips.bit_length() - 1
    rows = micro_count * row_count
    chunks = chunks_of(rows, row_count)
    sub = rows // chunks
    tall = sub * dp_count
    half, own = tall // 2, tall // mp_count
    ff_tile, out_tile = min(512, ff), min(256, width)
    low, f32 = jnp.bfloat16, jnp.float32

    families = {
        "swap": chunks * (chips - 1) * 2,
        "swap_pair": chunks,
        "lend": chunks * (chips - 1),
        "pair_a": chunks,
        "pair_b": chunks,
        "cross_a": chunks * hops,
        "cross_b": chunks * hops,
        "hidden": chunks,
        "slope": chunks,
        "stats": chunks,
        "sums": chunks * (mp_count - 1),
        "far": chunks,
        "direct": mp_count - 1,
        "onward": (chunks - 1) * (mp_count - 1),
        "away": chunks * mp_count * (chips - 1),
        "give": chunks * mp_count,
        "forward": chunks * mp_count * (chips - 1),
    }
    names = list(families)

    def kernel(act_ref, cot_ref, gain_ref, up_ref, down_ref, hid_out, grad_out, *refs):
        refs = list(refs)
        take = lambda n: [refs.pop(0) for _ in range(n)]
        up, down, start, gained, relayed = take(5)
        prod_a, prod_b, pair_a, pair_b, cross_a, cross_b = take(6)
        hid, slope, stats, branch, landed, ready = take(6)
        local_sem = take(1)[0]
        sems = {name: take(2) for name in names}

        me, mp_no = lax.axis_index("dp"), lax.axis_index("mp")
        section = lax.axis_index("section")
        chip, core = me // 2, lax.rem(me, 2)
        partner = {"dp": chip * 2 + 1 - core}
        parity = lax.rem(mp_no, 2)
        neighbour = mp_no + 1 - 2 * parity
        ring = [lax.rem(mp_no + step, mp_count) for step in range(mp_count)]
        origin = [lax.rem(mp_no + mp_count - step, mp_count) for step in range(mp_count)]
        far = [{"section": 1 - section, "mp": ring[step]} for step in range(mp_count)]
        dp_ring = [lax.rem(me + step, dp_count) for step in range(dp_count)]
        stage_a = (prod_a, pair_a, cross_a, "pair_a", "cross_a")
        stage_b = (prod_b, pair_b, cross_b, "pair_b", "cross_b")
        my_half = pl.ds(pl.multiple_of(core * half, half), half)
        other_half = pl.ds(pl.multiple_of((1 - core) * half, half), half)
        my_rows = pl.ds(pl.multiple_of(me * sub, sub), sub)
        owned = lambda z: pl.ds(pl.multiple_of(z * own, own), own)
        ext = pl.ds(ff, 128)

        def remote(name, at, src, dst, device):
            send, recv = sems[name]
            return pltpu.make_async_remote_copy(
                src_ref=src,
                dst_ref=dst,
                send_sem=send.at[at],
                recv_sem=recv.at[at],
                device_id=device,
                device_id_type=MESH,
            )

        def rows_of(ref, k, column_block):
            return ref.at[
                (k * sub) // row_count,
                pl.ds((k * sub) % row_count, sub),
                pl.ds(pl.multiple_of(column_block * width, width), width),
            ]

        def swap_copy(ref, k, step, to_core):
            other = lax.rem(chip + step, chips) * 2 + to_core
            return remote(
                "swap",
                (k * (chips - 1) + step - 1) * 2 + to_core,
                rows_of(ref, k, other),
                start.at[k, my_rows],
                {"dp": other},
            )

        def swap_pair_copy(ref, k):
            return remote(
                "swap_pair", k, rows_of(ref, k, partner["dp"]), start.at[k, my_rows], partner
            )

        def lend_copy(k, step):
            source = lax.rem(chip + chips - step, chips) * 2 + parity
            piece = start.at[k, pl.ds(pl.multiple_of(source * sub, sub), sub)]
            return remote("lend", k * (chips - 1) + step - 1, piece, piece, {"mp": neighbour})

        def swap_own(ref, k):
            return pltpu.make_async_copy(
                rows_of(ref, k, me), start.at[k, my_rows], local_sem.at[2 + k]
            )

        def pair_copy(stage, k):
            prod, pair, _, name, _ = stage
            return remote(name, k, prod.at[k, other_half], pair.at[k], partner)

        def cross_copy(stage, k, hop):
            prod, _, cross, _, name = stage
            bit = lax.rem(chip // (1 << hop), 2)
            other = chip + (1 << hop) * (1 - 2 * bit)
            return remote(
                name,
                k * hops + hop,
                prod.at[k, my_half],
                cross.at[k, hop],
                {"dp": other * 2 + core},
            )

        def half_copy(name, ref, k):
            return remote(name, k, ref.at[k, my_half], ref.at[k, my_half], partner)

        def sum_copy(k, step, columns):
            return remote(
                "sums",
                k * (mp_count - 1) + step - 1,
                branch.at[k, owned(ring[step]), pl.ds(0, columns)],
                landed.at[k, step - 1, :, pl.ds(0, columns)],
                {"mp": ring[step]},
            )

        def far_copy(k):
            return remote("far", k, ready.at[k], relayed.at[k, owned(mp_no)], far[0])

        def direct_copy(step):
            k = chunks - 1
            return remote(
                "direct", step - 1, ready.at[k], relayed.at[k, owned(mp_no)], far[step]
            )

        def onward_copy(k, step):
            rows_here = relayed.at[k, owned(mp_no)]
            return remote(
                "onward", k * (mp_count - 1) + step - 1, rows_here, rows_here, {"mp": ring[step]}
            )

        def away_copy(slab, k, piece, step):
            other = lax.rem(chip + step, chips)
            rows_here = owned(origin[piece])
            return remote(
                "away",
                (k * mp_count + piece) * (chips - 1) + step - 1,
                slab.at[k, rows_here],
                grad_out.at[me, k, rows_here],
                {"dp": other * 2 + core},
            )

        def give_copy(slab, k, piece):
            rows_here = owned(origin[piece])
            return remote(
                "give",
                k * mp_count + piece,
                slab.at[k, rows_here],
                grad_out.at[me, k, rows_here],
                partner,
            )

        def keep_copy(slab, k):
            return pltpu.make_async_copy(
                slab.at[k], grad_out.at[me, k], local_sem.at[2 + chunks + k]
            )

        def hid_copy(k):
            return pltpu.make_async_copy(hid.at[k], hid_out.at[k], local_sem.at[2 + 2 * chunks + k])

        def forward_copy(k, piece, step):
            source = lax.rem(chip + chips - step, chips)
            block = grad_out.at[source * 2 + core, k, owned(origin[piece])]
            return remote(
                "forward", (k * mp_count + piece) * (chips - 1) + step - 1, block, block, partner
            )

        def split(column):
            high = column.astype(low).astype(f32)
            lanes = lax.broadcasted_iota(jnp.int32, (column.shape[0], 128), 1)
            return jnp.where(lanes < 64, high, column - high).astype(low)

        def joined(block):
            wide = block.astype(f32)
            return wide[:, 0:1] + wide[:, 64:65]

        def each_tile(total, tile, body):
            @pl.loop(0, total // tile)
            def _(at):
                body(pl.ds(pl.multiple_of(at * tile, tile), tile))

        gain = gain_ref[:, pl.ds(pl.multiple_of(me * width, width), width)]

        def product(stage, k, source, weight, with_gain):
            prod = stage[0]
            wide = source[k].astype(f32)
            prod[k, :, ext] = split(jnp.sum(wide * wide, axis=1, keepdims=True))
            if with_gain:
                gained[...] = (wide * gain).astype(low)

            def tile(cols):
                left = gained[...] if with_gain else source[k]
                prod[k, :, cols] = matmul(left, weight[:, cols]).astype(low)

            each_tile(ff, ff_tile, tile)
            pair_copy(stage, k).start()

        def add_half(stage, k, other):
            prod = stage[0]

            def tile(cols):
                prod[k, my_half, cols] = (
                    prod[k, my_half, cols].astype(f32) + other[:, cols].astype(f32)
                ).astype(low)

            prod[k, my_half, ext] = split(joined(prod[k, my_half, ext]) + joined(other[:, ext]))
            each_tile(ff, ff_tile, tile)

        def fold(stage, k):
            pair_copy(stage, k).wait_recv()
            add_half(stage, k, stage[1].at[k])
            cross_copy(stage, k, 0).start()

        def crossed(stage, k):
            for hop in range(hops):
                cross_copy(stage, k, hop).wait_recv()
                if hop < hops - 1:
                    cross_copy(stage, k, hop).wait_send()
                    add_half(stage, k, stage[2].at[k, hop])
                    cross_copy(stage, k, hop + 1).start()

        def total_of(stage, k, cols):
            prod, _, cross = stage[:3]
            return prod[k, my_half, cols].astype(f32) + cross[k, hops - 1, :, cols].astype(f32)

        def inverse_rms(stage, k):
            prod, _, cross = stage[:3]
            squares = joined(prod[k, my_half, ext]) + joined(cross[k, hops - 1, :, ext])
            return lax.rsqrt(squares / model + norm_epsilon)

        def activate(k):
            crossed(stage_a, k)
            scale = inverse_rms(stage_a, k)

            def tile(cols):
                pre = total_of(stage_a, k, cols) * scale
                hid[k, my_half, cols] = (pre / (1.0 + jnp.exp(-pre))).astype(low)

            each_tile(ff, ff_tile, tile)
            half_copy("hidden", hid, k).start()

        def multiply_back(k, values, weight):
            def tile(cols):
                branch[k, :, cols] = matmul(values[k], weight[cols, :], 1, 1).astype(low)

            each_tile(width, out_tile, tile)

        def descend(k):
            half_copy("hidden", hid, k).wait_recv()
            hid_copy(k).start()
            multiply_back(k, hid, down)
            for step in range(1, mp_count):
                sum_copy(k, step, width).start()

        def reduced(k, columns):
            for step in range(1, mp_count):
                sum_copy(k, step, columns).wait_recv()
            cols = pl.ds(0, width)
            total = branch[k, owned(mp_no), cols].astype(f32)
            for step in range(1, mp_count):
                total += landed[k, step - 1, :, cols].astype(f32)
            return total

        def finish_forward(k):
            total = reduced(k, width)
            ready[k] = (start[k, owned(mp_no), :].astype(f32) + total).astype(low)
            send_ready(k)

        def backward(k):
            crossed(stage_a, k)
            crossed(stage_b, k)
            scale = inverse_rms(stage_b, k)

            def tile(at, dot):
                cols = pl.ds(pl.multiple_of(at * ff_tile, ff_tile), ff_tile)
                summed = total_of(stage_b, k, cols)
                pre = summed * scale
                gate = 1.0 / (1.0 + jnp.exp(-pre))
                hid[k, my_half, cols] = (pre * gate).astype(low)
                grad_pre = (
                    total_of(stage_a, k, cols) * (gate * (1.0 + pre * (1.0 - gate)))
                ).astype(low)
                slope[k, my_half, cols] = grad_pre
                return dot + jnp.sum(summed * grad_pre.astype(f32), axis=1, keepdims=True)

            dot = lax.fori_loop(0, ff // ff_tile, tile, jnp.zeros((half, 1), f32))
            stats[k, my_half, pl.ds(0, 128)] = jnp.broadcast_to(scale, (half, 128))
            stats[k, my_half, pl.ds(128, 128)] = jnp.broadcast_to(dot, (half, 128))
            half_copy("slope", slope, k).start()
            half_copy("stats", stats, k).start()

        def ascend(k):
            half_copy("stats", stats, k).wait_recv()
            branch[k, :, pl.ds(width, 128)] = split(stats[k, :, pl.ds(128, 128)][:, 0:1])
            half_copy("slope", slope, k).wait_recv()
            multiply_back(k, slope, up)
            for step in range(1, mp_count):
                sum_copy(k, step, width + 128).start()
            half_copy("hidden", hid, k).start()

        def finish_backward(k):
            total = reduced(k, width + 128)
            last = pl.ds(width, 128)
            dot = joined(branch[k, owned(mp_no), last])
            for step in range(1, mp_count):
                dot += joined(landed[k, step - 1, :, last])
            scale = stats[k, owned(mp_no), pl.ds(0, 128)][:, 0:1]
            values = relayed[k, owned(mp_no), :].astype(f32)
            ready[k] = (
                start[k, owned(mp_no), :].astype(f32)
                + scale * (gain * total)
                - values * ((scale * scale * scale / model) * dot)
            ).astype(low)
            send_ready(k)

        def send_ready(k):
            if k == chunks - 1:
                for step in range(1, mp_count):
                    direct_copy(step).start()
            far_copy(k).start()

        def pass_on(k):
            far_copy(k).wait_recv()
            if k < chunks - 1:
                for step in range(1, mp_count):
                    onward_copy(k, step).start()

        def arrived_from(k, step):
            copy = onward_copy(k, step) if k < chunks - 1 else direct_copy(step)
            copy.wait_recv()

        def arrived(k):
            for step in range(1, mp_count):
                arrived_from(k, step)

        def spread(slab, k, piece):
            for step in range(1, chips):
                away_copy(slab, k, piece, step).start()
            give_copy(slab, k, piece).start()

        def hand_over(slab, k):
            for piece in range(mp_count):
                for step in range(1, chips):
                    away_copy(slab, k, piece, step).wait_recv()
                    forward_copy(k, piece, step).start()

        def begin(ref):
            @pl.when(core == parity)
            def _():
                for k in range(chunks):
                    for step in range(1, chips):
                        for to_core in range(2):
                            swap_copy(ref, k, step, to_core).start()

            for k in range(chunks):
                swap_pair_copy(ref, k).start()
                swap_own(ref, k).start()

        def lend(ref, k):
            for step in range(1, chips):
                swap_copy(ref, k, step, core).wait_recv()
                lend_copy(k, step).start()

        def started(ref, k):
            if k == 0:
                lend(ref, 0)
            if k + 1 < chunks:
                lend(ref, k + 1)
            swap_own(ref, k).wait()
            swap_pair_copy(ref, k).wait_recv()
            for step in range(1, chips):
                lend_copy(k, step).wait_recv()

        def finish(ref, slab, stages, names_sent, columns):
            @pl.when(core == parity)
            def _():
                for k in range(chunks):
                    for step in range(1, chips):
                        for to_core in range(2):
                            swap_copy(ref, k, step, to_core).wait_send()

            for k in range(chunks):
                swap_pair_copy(ref, k).wait_send()
                for step in range(1, chips):
                    lend_copy(k, step).wait_send()
                for stage in stages:
                    pair_copy(stage, k).wait_send()
                    cross_copy(stage, k, hops - 1).wait_send()
                for name, buffer in names_sent:
                    half_copy(name, buffer, k).wait_send()
                for step in range(1, mp_count):
                    sum_copy(k, step, columns).wait_send()
                    if k < chunks - 1:
                        onward_copy(k, step).wait_send()
                    else:
                        direct_copy(step).wait_send()
                far_copy(k).wait_send()
                hid_copy(k).wait()
                keep_copy(slab, k).wait()
                for piece in range(mp_count):
                    give_copy(slab, k, piece).wait()
                    for step in range(1, chips):
                        away_copy(slab, k, piece, step).wait_send()
                        forward_copy(k, piece, step).wait()

        up_load = pltpu.make_async_copy(up_ref, up, local_sem.at[0])
        down_load = pltpu.make_async_copy(down_ref, down, local_sem.at[1])
        meet(
            [{"dp": dp_ring[step]} for step in range(1, dp_count)]
            + [{"mp": ring[step]} for step in range(1, mp_count)]
            + far
        )

        @pl.when(section == 0)
        def _():
            begin(act_ref)
            up_load.start()
            down_load.start()
            for slot in range(chunks + 1):
                if slot < chunks:
                    started(act_ref, slot)
                    if slot == 0:
                        up_load.wait()
                    product(stage_a, slot, start, up, True)
                if slot >= 1:
                    fold(stage_a, slot - 1)
            down_load.wait()
            for slot in range(chunks + 1):
                if slot < chunks:
                    activate(slot)
                    descend(slot)
                if slot >= 1:
                    finish_forward(slot - 1)
            for slot in range(chunks + 1):
                if slot < chunks - 1:
                    pass_on(slot)
                    spread(relayed, slot, 0)
                if slot >= 1:
                    for step in range(1, mp_count):
                        arrived_from(slot - 1, step)
                        spread(relayed, slot - 1, step)
                    keep_copy(relayed, slot - 1).start()
                if slot == chunks - 1:
                    pass_on(slot)
                    spread(relayed, slot, 0)
                if slot >= 2:
                    hand_over(relayed, slot - 2)
            hand_over(relayed, chunks - 1)
            finish(act_ref, relayed, [stage_a], [("hidden", hid)], width)

        @pl.when(section != 0)
        def _():
            begin(cot_ref)
            down_load.start()
            up_load.start()
            for slot in range(chunks + 1):
                if slot < chunks:
                    started(cot_ref, slot)
                    if slot == 0:
                        down_load.wait()
                    product(stage_a, slot, start, down, False)
                if 0 <= slot - 1 < chunks:
                    fold(stage_a, slot - 1)
            up_load.wait()
            pass_on(0)
            for slot in range(chunks + 3):
                if slot + 1 < chunks:
                    pass_on(slot + 1)
                if slot < chunks:
                    arrived(slot)
                    product(stage_b, slot, relayed, up, True)
                if 0 <= slot - 2 < chunks:
                    ascend(slot - 2)
                if slot < chunks:
                    fold(stage_b, slot)
                if 0 <= slot - 3 < chunks:
                    finish_backward(slot - 3)
                if 0 <= slot - 1 < chunks:
                    backward(slot - 1)
                if slot == chunks:
                    for k in range(chunks):
                        for piece in range(mp_count):
                            spread(start, k, piece)
                        keep_copy(start, k).start()
            for k in range(chunks):
                half_copy("hidden", hid, k).wait_recv()
                hid_copy(k).start()
            for k in range(chunks):
                hand_over(start, k)
            finish(
                cot_ref,
                start,
                [stage_a, stage_b],
                [("hidden", hid), ("slope", slope), ("stats", stats)],
                width + 128,
            )

    dma = pltpu.SemaphoreType.DMA
    vmem = pltpu.VMEM
    scratch = [
        vmem((width, ff), low),
        vmem((width, ff), low),
        vmem((chunks, tall, width), low),
        vmem((tall, width), low),
        vmem((chunks, tall, width), low),
        vmem((chunks, tall, ff + 128), low),
        vmem((chunks, tall, ff + 128), low),
        vmem((chunks, half, ff + 128), low),
        vmem((chunks, half, ff + 128), low),
        vmem((chunks, hops, half, ff + 128), low),
        vmem((chunks, hops, half, ff + 128), low),
        vmem((chunks, tall, ff), low),
        vmem((chunks, tall, ff), low),
        vmem((chunks, tall, 256), f32),
        vmem((chunks, tall, width + 128), low),
        vmem((chunks, mp_count - 1, own, width + 128), low),
        vmem((chunks, own, width), low),
        dma((2 + 3 * chunks,)),
    ]
    for name in names:
        scratch += [dma((families[name],)), dma((families[name],))]
    return pl.pallas_call(
        kernel,
        out_shape=[
            jax.ShapeDtypeStruct((chunks, tall, ff), low),
            jax.ShapeDtypeStruct((dp_count, chunks, tall, width), low),
        ],
        in_specs=[
            pl.BlockSpec(memory_space=pltpu.HBM),
            pl.BlockSpec(memory_space=pltpu.HBM),
            pl.BlockSpec(memory_space=pltpu.VMEM),
            pl.BlockSpec(memory_space=pltpu.HBM),
            pl.BlockSpec(memory_space=pltpu.HBM),
        ],
        out_specs=[pl.BlockSpec(memory_space=pl.ANY)] * 2,
        scratch_shapes=scratch,
        compiler_params=pltpu.CompilerParams(
            collective_id=0, has_side_effects=True, vmem_limit_bytes=VMEM_LIMIT
        ),
        name="relay",
    )(activations, cotangent, gain_rows, w_up, w_down)


def inverse_root(matrix):
    low = jnp.bfloat16
    order = matrix.shape[-1]
    on_diagonal = lax.broadcasted_iota(jnp.int32, (order, order), 0) == lax.broadcasted_iota(
        jnp.int32, (order, order), 1
    )
    identity = jnp.where(on_diagonal, 1.0, 0.0).astype(jnp.float32)
    shifted = matrix + ridge_shift * identity
    norm_sq = jnp.sum(jnp.sum(shifted * shifted, axis=1, keepdims=True), axis=0, keepdims=True)
    factor = 2.5 / jnp.sqrt(norm_sq)
    moment = factor * shifted
    moment_low = moment.astype(low)
    moment_sq = matmul(moment_low, moment_low)
    square = (1.5625 * identity - 0.625 * moment + 0.0625 * moment_sq).astype(low)
    stepped = (1.25 * moment - 0.25 * moment_sq).astype(low)
    third = matmul(square, stepped).astype(low)
    fifth = matmul(square, third)
    scale = jnp.sqrt(jnp.sqrt(factor))
    return scale * (1.5625 * identity - 0.3125 * moment - 0.25 * fifth)


def gram(values, dim):
    middle = values.shape[0] // 2
    first = values[:middle] if dim == 1 else values[:, :middle]
    second = values[middle:] if dim == 1 else values[:, middle:]
    top = matmul(first, values, dim, dim)
    low_left = top[:, middle:].T
    return jnp.concatenate(
        [top, jnp.concatenate([low_left, matmul(second, second, dim, dim)], axis=1)], axis=0
    )


def precondition(hidden, grads, grams_and_roots, owner_slot, eighth, refresh_phase, block_cols):
    slots = grams_and_roots[0].shape[0]
    tokens, shard_ff = hidden.shape
    width = grads.shape[2]
    block_rows = shard_ff // BLK
    scale = 1.0 / math.sqrt(tokens)
    pieces = max(BLK // width, 1)
    per = max(width // BLK, 1)

    def kernel(
        owner_ref, eighth_ref, phase_ref, hid_ref, grad_ref, gl_ref, gr_ref, rl_ref, rr_ref,
        gl_out, gr_out, rl_out, rr_out, up_out,
        hid, dy, gl, gr, rl, rr, block, due, sem,
    ):
        slot = pl.program_id(0)

        def loads(at):
            row, col = lax.div(block[at], block_cols), lax.rem(block[at], block_cols)
            copy = lambda src, dst, n: pltpu.make_async_copy(src, dst, sem.at[at, n])
            copies = [
                copy(hid_ref.at[:, pl.ds(pl.multiple_of(row * BLK, BLK), BLK)], hid.at[at], 0)
            ]
            if width >= BLK:
                first = pl.multiple_of(lax.rem(col, per) * BLK, BLK)
                source = grad_ref.at[lax.div(col, per), :, pl.ds(first, BLK)]
                copies.append(copy(source, dy.at[at], 1))
            else:
                for piece in range(pieces):
                    target = dy.at[at, :, pl.ds(piece * width, width)]
                    copies.append(copy(grad_ref.at[col * pieces + piece], target, 1 + piece))
            sources = ((gl_ref, gl), (gr_ref, gr), (rl_ref, rl), (rr_ref, rr))
            for n, (source, target) in enumerate(sources):
                copies.append(copy(source.at[at], target.at[at], 1 + pieces + n))
            return copies

        @pl.when(slot == 0)
        def _():
            section, mp_no = lax.axis_index("section"), lax.axis_index("mp")
            base = (lax.axis_index("dp") * lax.axis_size("mp") + mp_no) * slots
            phase = lax.rem(phase_ref[0], 8)

            for at in range(block_rows * block_cols):
                row, col = mp_no * block_rows + at // block_cols, at % block_cols
                place = owner_ref[section, col, row] - base
                place = jnp.where((place >= 0) & (place < slots), place, slots)
                block[place] = at
                due[place] = jnp.where(eighth_ref[section, col, row] == phase, 1, 0)

            @pl.loop(0, slots)
            def _(at):
                for copy in loads(at):
                    copy.start()

        copies = loads(slot)
        for copy in copies[: 1 + pieces]:
            copy.wait()
        grad_low = (matmul(hid[slot], dy[slot], 0, 0) * scale).astype(jnp.bfloat16)
        for copy in copies[1 + pieces :]:
            copy.wait()
        gl_out[0] = decay_rate * gl[slot] + gram(grad_low, 1) * (1.0 / BLK)
        gr_out[0] = decay_rate * gr[slot] + gram(grad_low, 0) * (1.0 / BLK)

        @pl.when(due[slot] != 0)
        def _():
            rl_out[0] = inverse_root(gl_out[0]).astype(jnp.bfloat16)
            rr_out[0] = inverse_root(gr_out[0]).astype(jnp.bfloat16)

        @pl.when(due[slot] == 0)
        def _():
            rl_out[0] = rl[slot]
            rr_out[0] = rr[slot]

        right_part = matmul(grad_low, rr_out[0]).astype(jnp.bfloat16)
        up_out[0] = matmul(rl_out[0], right_part).astype(jnp.bfloat16)

    low, f32 = jnp.bfloat16, jnp.float32
    square_spec = pl.BlockSpec((1, BLK, BLK), lambda s: (s, 0, 0))
    square = lambda dtype: jax.ShapeDtypeStruct((slots, BLK, BLK), dtype)
    return pl.pallas_call(
        kernel,
        grid=(slots,),
        in_specs=[pl.BlockSpec(memory_space=pltpu.SMEM)] * 3
        + [pl.BlockSpec(memory_space=pl.ANY)] * 6,
        out_specs=[square_spec] * 5,
        out_shape=[square(f32), square(f32), square(low), square(low), square(low)],
        scratch_shapes=[
            pltpu.VMEM((slots, tokens, BLK), low),
            pltpu.VMEM((slots, tokens, BLK), low),
            pltpu.VMEM((slots, BLK, BLK), f32),
            pltpu.VMEM((slots, BLK, BLK), f32),
            pltpu.VMEM((slots, BLK, BLK), low),
            pltpu.VMEM((slots, BLK, BLK), low),
            pltpu.SMEM((slots + 1,), jnp.int32),
            pltpu.SMEM((slots + 1,), jnp.int32),
            pltpu.SemaphoreType.DMA((slots, 5 + pieces)),
        ],
        compiler_params=pltpu.CompilerParams(
            dimension_semantics=("arbitrary",), vmem_limit_bytes=VMEM_LIMIT
        ),
        name="precondition",
    )(owner_slot, eighth, refresh_phase, hidden, grads, *grams_and_roots)


def on_device(
    activations,
    cotangent,
    norm_gain,
    w_up,
    w_down,
    gram_left,
    gram_right,
    root_left,
    root_right,
    owner_slot,
    eighth,
    refresh_phase,
):
    width, shard_ff = w_up.shape[1:]
    hidden, grads = relay(activations, cotangent, norm_gain, w_up[0], w_down[0])
    results = precondition(
        hidden.reshape(-1, shard_ff),
        grads.reshape(grads.shape[0], -1, width),
        [x[0] for x in (gram_left, gram_right, root_left, root_right)],
        owner_slot.swapaxes(1, 2),
        eighth.swapaxes(1, 2),
        refresh_phase,
        activations.shape[2] // BLK,
    )
    return tuple(result[None] for result in results)


def solution(mesh):
    return jax.shard_map(
        on_device,
        mesh=mesh,
        in_specs=(
            P(None, "dp", None),
            P(None, "dp", None),
            P("section", None),
            P("section", "dp", "mp"),
            P("section", "dp", "mp"),
            P("section", ("dp", "mp"), None, None),
            P("section", ("dp", "mp"), None, None),
            P("section", ("dp", "mp"), None, None),
            P("section", ("dp", "mp"), None, None),
            P(),
            P(),
            P(),
        ),
        out_specs=(
            P("section", ("dp", "mp"), None, None),
            P("section", ("dp", "mp"), None, None),
            P("section", ("dp", "mp"), None, None),
            P("section", ("dp", "mp"), None, None),
            P("section", ("dp", "mp"), None, None),
        ),
        check_vma=False,
    )
```

```python
import math

import jax
import jax.numpy as jnp
from jax import lax
from jax.experimental import pallas as pl
from jax.experimental.pallas import tpu as pltpu
from jax.sharding import PartitionSpec as P

BLK = 512
MESH = pl.DeviceIdType.MESH
VMEM_LIMIT = 60 * 1024 * 1024

norm_epsilon = 1e-05
decay_rate = 0.9
ridge_shift = 0.001


def meet(devices):
    barrier = pltpu.get_barrier_semaphore()
    for device in devices:
        pl.semaphore_signal(barrier, inc=1, device_id=device, device_id_type=MESH)
    pl.semaphore_wait(barrier, len(devices))


def chunks_of(rows, row_count):
    fits = lambda n: rows % n == 0 and row_count % (rows // n) == 0 and (rows // n) % 16 == 0
    return max([n for n in (1, 2, 4) if fits(n)])


def matmul(left, right, left_dim=1, right_dim=0):
    return lax.dot_general(
        left, right, (((left_dim,), (right_dim,)), ((), ())), preferred_element_type=jnp.float32
    )


def relay(activations, cotangent, gain_rows, w_up, w_down):
    micro_count, row_count, model = activations.shape
    width, ff = w_up.shape
    dp_count, mp_count = lax.axis_size("dp"), lax.axis_size("mp")
    chips = dp_count // 2
    hops = chips.bit_length() - 1
    rows = micro_count * row_count
    chunks = chunks_of(rows, row_count)
    sub = rows // chunks
    tall = sub * dp_count
    half, own = tall // 2, tall // mp_count
    ff_tile, out_tile = min(512, ff), min(256, width)
    low, f32 = jnp.bfloat16, jnp.float32

    families = {
        "swap": chunks * (chips - 1) * 2,
        "swap_pair": chunks,
        "lend": chunks * (chips - 1),
        "pair_a": chunks,
        "pair_b": chunks,
        "cross_a": chunks * hops,
        "cross_b": chunks * hops,
        "hidden": chunks,
        "slope": chunks,
        "stats": chunks,
        "sums": chunks * (mp_count - 1),
        "far": chunks,
        "direct": mp_count - 1,
        "onward": (chunks - 1) * (mp_count - 1),
        "away": chunks * mp_count * (chips - 1),
        "give": chunks * mp_count,
        "forward": chunks * mp_count * (chips - 1),
    }
    names = list(families)
    sent_once = ("swap_pair", "pair_a", "pair_b", "hidden", "slope", "stats")
    sent_once += ("sums", "far", "onward", "away", "give", "forward")
    landed_once = ("give", "forward")

    def kernel(act_ref, cot_ref, gain_ref, up_ref, down_ref, hid_out, grad_out, *refs):
        refs = list(refs)
        take = lambda n: [refs.pop(0) for _ in range(n)]
        up, down, start, gained, relayed = take(5)
        prod_a, prod_b, pair_a, pair_b, cross_a, cross_b = take(6)
        hid, slope, stats, branch, landed, ready = take(6)
        local_sem = take(1)[0]
        sems = {name: take(2) for name in names}

        me, mp_no = lax.axis_index("dp"), lax.axis_index("mp")
        section = lax.axis_index("section")
        chip, core = me // 2, lax.rem(me, 2)
        partner = {"dp": chip * 2 + 1 - core}
        parity = lax.rem(mp_no, 2)
        neighbour = mp_no + 1 - 2 * parity
        ring = [lax.rem(mp_no + step, mp_count) for step in range(mp_count)]
        origin = [lax.rem(mp_no + mp_count - step, mp_count) for step in range(mp_count)]
        far = [{"section": 1 - section, "mp": ring[step]} for step in range(mp_count)]
        dp_ring = [lax.rem(me + step, dp_count) for step in range(dp_count)]
        stage_a = (prod_a, pair_a, cross_a, "pair_a", "cross_a")
        stage_b = (prod_b, pair_b, cross_b, "pair_b", "cross_b")
        my_half = pl.ds(pl.multiple_of(core * half, half), half)
        other_half = pl.ds(pl.multiple_of((1 - core) * half, half), half)
        my_rows = pl.ds(pl.multiple_of(me * sub, sub), sub)
        owned = lambda z: pl.ds(pl.multiple_of(z * own, own), own)
        ext = pl.ds(ff, 128)

        def remote(name, at, src, dst, device):
            send, recv = sems[name]
            return pltpu.make_async_remote_copy(
                src_ref=src,
                dst_ref=dst,
                send_sem=send.at[0 if name in sent_once else at],
                recv_sem=recv.at[0 if name in landed_once else at],
                device_id=device,
                device_id_type=MESH,
            )

        def rows_of(ref, k, column_block):
            return ref.at[
                (k * sub) // row_count,
                pl.ds((k * sub) % row_count, sub),
                pl.ds(pl.multiple_of(column_block * width, width), width),
            ]

        def swap_copy(ref, k, step, to_core):
            other = lax.rem(chip + step, chips) * 2 + to_core
            return remote(
                "swap",
                (k * (chips - 1) + step - 1) * 2 + to_core,
                rows_of(ref, k, other),
                start.at[k, my_rows],
                {"dp": other},
            )

        def swap_pair_copy(ref, k):
            return remote(
                "swap_pair", k, rows_of(ref, k, partner["dp"]), start.at[k, my_rows], partner
            )

        def lend_copy(k, step):
            source = lax.rem(chip + chips - step, chips) * 2 + parity
            piece = start.at[k, pl.ds(pl.multiple_of(source * sub, sub), sub)]
            return remote("lend", k * (chips - 1) + step - 1, piece, piece, {"mp": neighbour})

        def swap_own(ref, k):
            return pltpu.make_async_copy(
                rows_of(ref, k, me), start.at[k, my_rows], local_sem.at[2 + k]
            )

        def pair_copy(stage, k):
            prod, pair, _, name, _ = stage
            return remote(name, k, prod.at[k, other_half], pair.at[k], partner)

        def cross_copy(stage, k, hop):
            prod, _, cross, _, name = stage
            bit = lax.rem(chip // (1 << hop), 2)
            other = chip + (1 << hop) * (1 - 2 * bit)
            return remote(
                name,
                k * hops + hop,
                prod.at[k, my_half],
                cross.at[k, hop],
                {"dp": other * 2 + core},
            )

        def half_copy(name, ref, k):
            return remote(name, k, ref.at[k, my_half], ref.at[k, my_half], partner)

        def sum_copy(k, step, columns):
            return remote(
                "sums",
                k * (mp_count - 1) + step - 1,
                branch.at[k, owned(ring[step]), pl.ds(0, columns)],
                landed.at[k, step - 1, :, pl.ds(0, columns)],
                {"mp": ring[step]},
            )

        def far_copy(k):
            return remote("far", k, ready.at[k], relayed.at[k, owned(mp_no)], far[0])

        def direct_copy(step):
            k = chunks - 1
            return remote(
                "direct", step - 1, ready.at[k], relayed.at[k, owned(mp_no)], far[step]
            )

        def onward_copy(k, step):
            rows_here = relayed.at[k, owned(mp_no)]
            return remote(
                "onward", k * (mp_count - 1) + step - 1, rows_here, rows_here, {"mp": ring[step]}
            )

        def away_copy(slab, k, piece, step):
            other = lax.rem(chip + step, chips)
            rows_here = owned(origin[piece])
            return remote(
                "away",
                (k * mp_count + piece) * (chips - 1) + step - 1,
                slab.at[k, rows_here],
                grad_out.at[me, k, rows_here],
                {"dp": other * 2 + core},
            )

        def give_copy(slab, k, piece):
            rows_here = owned(origin[piece])
            return remote(
                "give",
                k * mp_count + piece,
                slab.at[k, rows_here],
                grad_out.at[me, k, rows_here],
                partner,
            )

        def keep_copy(slab, k):
            return pltpu.make_async_copy(
                slab.at[k], grad_out.at[me, k], local_sem.at[2 + chunks + k]
            )

        def hid_copy(k):
            return pltpu.make_async_copy(hid.at[k], hid_out.at[k], local_sem.at[2 + 2 * chunks + k])

        def forward_copy(k, piece, step):
            source = lax.rem(chip + chips - step, chips)
            block = grad_out.at[source * 2 + core, k, owned(origin[piece])]
            return remote(
                "forward", (k * mp_count + piece) * (chips - 1) + step - 1, block, block, partner
            )

        def split(column):
            high = column.astype(low).astype(f32)
            lanes = lax.broadcasted_iota(jnp.int32, (column.shape[0], 128), 1)
            return jnp.where(lanes < 64, high, column - high).astype(low)

        def joined(block):
            wide = block.astype(f32)
            return wide[:, 0:1] + wide[:, 64:65]

        def each_tile(total, tile, body):
            @pl.loop(0, total // tile)
            def _(at):
                body(pl.ds(pl.multiple_of(at * tile, tile), tile))

        gain = gain_ref[:, pl.ds(pl.multiple_of(me * width, width), width)]

        def product(stage, k, source, weight, with_gain):
            prod = stage[0]
            wide = source[k].astype(f32)
            prod[k, :, ext] = split(jnp.sum(wide * wide, axis=1, keepdims=True))
            if with_gain:
                gained[...] = (wide * gain).astype(low)

            def tile(cols):
                left = gained[...] if with_gain else source[k]
                prod[k, :, cols] = matmul(left, weight[:, cols]).astype(low)

            each_tile(ff, ff_tile, tile)
            pair_copy(stage, k).start()

        def add_half(stage, k, other):
            prod = stage[0]

            def tile(cols):
                prod[k, my_half, cols] = (
                    prod[k, my_half, cols].astype(f32) + other[:, cols].astype(f32)
                ).astype(low)

            prod[k, my_half, ext] = split(joined(prod[k, my_half, ext]) + joined(other[:, ext]))
            each_tile(ff, ff_tile, tile)

        def fold(stage, k):
            pair_copy(stage, k).wait_recv()
            add_half(stage, k, stage[1].at[k])
            cross_copy(stage, k, 0).start()

        def crossed(stage, k):
            for hop in range(hops):
                cross_copy(stage, k, hop).wait_recv()
                if hop < hops - 1:
                    cross_copy(stage, k, hop).wait_send()
                    add_half(stage, k, stage[2].at[k, hop])
                    cross_copy(stage, k, hop + 1).start()

        def total_of(stage, k, cols):
            prod, _, cross = stage[:3]
            return prod[k, my_half, cols].astype(f32) + cross[k, hops - 1, :, cols].astype(f32)

        def inverse_rms(stage, k):
            prod, _, cross = stage[:3]
            squares = joined(prod[k, my_half, ext]) + joined(cross[k, hops - 1, :, ext])
            return lax.rsqrt(squares / model + norm_epsilon)

        def activate(k):
            crossed(stage_a, k)
            scale = inverse_rms(stage_a, k)

            def tile(cols):
                pre = total_of(stage_a, k, cols) * scale
                hid[k, my_half, cols] = (pre / (1.0 + jnp.exp(-pre))).astype(low)

            each_tile(ff, ff_tile, tile)
            half_copy("hidden", hid, k).start()

        def multiply_back(k, values, weight):
            def tile(cols):
                branch[k, :, cols] = matmul(values[k], weight[cols, :], 1, 1).astype(low)

            each_tile(width, out_tile, tile)

        def descend(k):
            half_copy("hidden", hid, k).wait_recv()
            hid_copy(k).start()
            multiply_back(k, hid, down)
            for step in range(1, mp_count):
                sum_copy(k, step, width).start()

        def reduced(k, columns):
            for step in range(1, mp_count):
                sum_copy(k, step, columns).wait_recv()
            cols = pl.ds(0, width)
            total = branch[k, owned(mp_no), cols].astype(f32)
            for step in range(1, mp_count):
                total += landed[k, step - 1, :, cols].astype(f32)
            return total

        def finish_forward(k):
            total = reduced(k, width)
            ready[k] = (start[k, owned(mp_no), :].astype(f32) + total).astype(low)
            send_ready(k)

        def backward(k):
            crossed(stage_a, k)
            crossed(stage_b, k)
            scale = inverse_rms(stage_b, k)

            def tile(at, dot):
                cols = pl.ds(pl.multiple_of(at * ff_tile, ff_tile), ff_tile)
                summed = total_of(stage_b, k, cols)
                pre = summed * scale
                gate = 1.0 / (1.0 + jnp.exp(-pre))
                hid[k, my_half, cols] = (pre * gate).astype(low)
                grad_pre = (
                    total_of(stage_a, k, cols) * (gate * (1.0 + pre * (1.0 - gate)))
                ).astype(low)
                slope[k, my_half, cols] = grad_pre
                return dot + jnp.sum(summed * grad_pre.astype(f32), axis=1, keepdims=True)

            dot = lax.fori_loop(0, ff // ff_tile, tile, jnp.zeros((half, 1), f32))
            stats[k, my_half, pl.ds(0, 128)] = jnp.broadcast_to(scale, (half, 128))
            stats[k, my_half, pl.ds(128, 128)] = jnp.broadcast_to(dot, (half, 128))
            half_copy("slope", slope, k).start()
            half_copy("stats", stats, k).start()

        def ascend(k):
            half_copy("stats", stats, k).wait_recv()
            branch[k, :, pl.ds(width, 128)] = split(stats[k, :, pl.ds(128, 128)][:, 0:1])
            half_copy("slope", slope, k).wait_recv()
            multiply_back(k, slope, up)
            for step in range(1, mp_count):
                sum_copy(k, step, width + 128).start()
            half_copy("hidden", hid, k).start()

        def finish_backward(k):
            total = reduced(k, width + 128)
            last = pl.ds(width, 128)
            dot = joined(branch[k, owned(mp_no), last])
            for step in range(1, mp_count):
                dot += joined(landed[k, step - 1, :, last])
            scale = stats[k, owned(mp_no), pl.ds(0, 128)][:, 0:1]
            values = relayed[k, owned(mp_no), :].astype(f32)
            ready[k] = (
                start[k, owned(mp_no), :].astype(f32)
                + scale * (gain * total)
                - values * ((scale * scale * scale / model) * dot)
            ).astype(low)
            send_ready(k)

        def send_ready(k):
            if k == chunks - 1:
                for step in range(1, mp_count):
                    direct_copy(step).start()
            far_copy(k).start()

        def pass_on(k):
            far_copy(k).wait_recv()
            if k < chunks - 1:
                for step in range(1, mp_count):
                    onward_copy(k, step).start()

        def arrived_from(k, step):
            copy = onward_copy(k, step) if k < chunks - 1 else direct_copy(step)
            copy.wait_recv()

        def arrived(k):
            for step in range(1, mp_count):
                arrived_from(k, step)

        def spread(slab, k, piece):
            for step in range(1, chips):
                away_copy(slab, k, piece, step).start()
            give_copy(slab, k, piece).start()

        def hand_over(slab, k):
            for piece in range(mp_count):
                for step in range(1, chips):
                    away_copy(slab, k, piece, step).wait_recv()
                    forward_copy(k, piece, step).start()

        def begin(ref):
            @pl.when(core == parity)
            def _():
                for k in range(chunks):
                    for step in range(1, chips):
                        for to_core in range(2):
                            swap_copy(ref, k, step, to_core).start()

            for k in range(chunks):
                swap_pair_copy(ref, k).start()
                swap_own(ref, k).start()

        def lend(ref, k):
            for step in range(1, chips):
                swap_copy(ref, k, step, core).wait_recv()
                lend_copy(k, step).start()

        def started(ref, k):
            if k == 0:
                lend(ref, 0)
            if k + 1 < chunks:
                lend(ref, k + 1)
            swap_own(ref, k).wait()
            swap_pair_copy(ref, k).wait_recv()
            for step in range(1, chips):
                lend_copy(k, step).wait_recv()

        def finish(ref, slab, stages, names_sent, columns):
            @pl.when(core == parity)
            def _():
                for k in range(chunks):
                    for step in range(1, chips):
                        for to_core in range(2):
                            swap_copy(ref, k, step, to_core).wait_send()

            whole = lambda name, ref: remote(name, 0, ref, ref, partner)
            whole("swap_pair", start.at[:, my_rows]).wait_send()
            for stage in stages:
                whole(stage[3], stage[0].at[:, other_half]).wait_send()
            for name, buffer in names_sent:
                whole(name, buffer.at[:, my_half]).wait_send()
            others = pl.ds(0, own * (mp_count - 1))
            whole("sums", branch.at[:, others, pl.ds(0, columns)]).wait_send()
            if chunks > 1:
                whole("onward", relayed.at[pl.ds(0, chunks - 1), others]).wait_send()
            whole("far", ready).wait_send()
            for step in range(1, mp_count):
                direct_copy(step).wait_send()
            for k in range(chunks):
                for step in range(1, chips):
                    lend_copy(k, step).wait_send()
                for stage in stages:
                    cross_copy(stage, k, hops - 1).wait_send()
                hid_copy(k).wait()
                keep_copy(slab, k).wait()
            whole("away", grad_out.at[pl.ds(0, chips - 1)]).wait_send()
            whole("give", grad_out.at[me]).wait()
            whole("forward", grad_out.at[pl.ds(0, chips - 1)]).wait()

        up_load = pltpu.make_async_copy(up_ref, up, local_sem.at[0])
        down_load = pltpu.make_async_copy(down_ref, down, local_sem.at[1])
        meet(
            [{"dp": dp_ring[step]} for step in range(1, dp_count)]
            + [{"mp": ring[step]} for step in range(1, mp_count)]
            + far
        )

        @pl.when(section == 0)
        def _():
            begin(act_ref)
            up_load.start()
            down_load.start()
            for slot in range(chunks + 1):
                if slot < chunks:
                    started(act_ref, slot)
                    if slot == 0:
                        up_load.wait()
                    product(stage_a, slot, start, up, True)
                if slot >= 1:
                    fold(stage_a, slot - 1)
            down_load.wait()
            for slot in range(chunks + 1):
                if slot < chunks:
                    activate(slot)
                    descend(slot)
                if slot >= 1:
                    finish_forward(slot - 1)
            for slot in range(chunks + 1):
                if slot < chunks - 1:
                    pass_on(slot)
                    spread(relayed, slot, 0)
                if slot >= 1:
                    for step in range(1, mp_count):
                        arrived_from(slot - 1, step)
                        spread(relayed, slot - 1, step)
                    keep_copy(relayed, slot - 1).start()
                if slot == chunks - 1:
                    pass_on(slot)
                    spread(relayed, slot, 0)
                if slot >= 2:
                    hand_over(relayed, slot - 2)
            hand_over(relayed, chunks - 1)
            finish(act_ref, relayed, [stage_a], [("hidden", hid)], width)

        @pl.when(section != 0)
        def _():
            begin(cot_ref)
            down_load.start()
            up_load.start()
            for slot in range(chunks + 1):
                if slot < chunks:
                    started(cot_ref, slot)
                    if slot == 0:
                        down_load.wait()
                    product(stage_a, slot, start, down, False)
                if 0 <= slot - 1 < chunks:
                    fold(stage_a, slot - 1)
            up_load.wait()
            pass_on(0)
            for slot in range(chunks + 3):
                if slot + 1 < chunks:
                    pass_on(slot + 1)
                if slot < chunks:
                    arrived(slot)
                    product(stage_b, slot, relayed, up, True)
                if 0 <= slot - 2 < chunks:
                    ascend(slot - 2)
                if slot < chunks:
                    fold(stage_b, slot)
                if 0 <= slot - 3 < chunks:
                    finish_backward(slot - 3)
                if 0 <= slot - 1 < chunks:
                    backward(slot - 1)
                if slot == chunks:
                    for k in range(chunks):
                        for piece in range(mp_count):
                            spread(start, k, piece)
                        keep_copy(start, k).start()
            for k in range(chunks):
                half_copy("hidden", hid, k).wait_recv()
                hid_copy(k).start()
            for k in range(chunks):
                hand_over(start, k)
            finish(
                cot_ref,
                start,
                [stage_a, stage_b],
                [("hidden", hid), ("slope", slope), ("stats", stats)],
                width + 128,
            )

    dma = pltpu.SemaphoreType.DMA
    vmem = pltpu.VMEM
    scratch = [
        vmem((width, ff), low),
        vmem((width, ff), low),
        vmem((chunks, tall, width), low),
        vmem((tall, width), low),
        vmem((chunks, tall, width), low),
        vmem((chunks, tall, ff + 128), low),
        vmem((chunks, tall, ff + 128), low),
        vmem((chunks, half, ff + 128), low),
        vmem((chunks, half, ff + 128), low),
        vmem((chunks, hops, half, ff + 128), low),
        vmem((chunks, hops, half, ff + 128), low),
        vmem((chunks, tall, ff), low),
        vmem((chunks, tall, ff), low),
        vmem((chunks, tall, 256), f32),
        vmem((chunks, tall, width + 128), low),
        vmem((chunks, mp_count - 1, own, width + 128), low),
        vmem((chunks, own, width), low),
        dma((2 + 3 * chunks,)),
    ]
    for name in names:
        scratch += [
            dma((1 if name in sent_once else families[name],)),
            dma((1 if name in landed_once else families[name],)),
        ]
    return pl.pallas_call(
        kernel,
        out_shape=[
            jax.ShapeDtypeStruct((chunks, tall, ff), low),
            jax.ShapeDtypeStruct((dp_count, chunks, tall, width), low),
        ],
        in_specs=[
            pl.BlockSpec(memory_space=pltpu.HBM),
            pl.BlockSpec(memory_space=pltpu.HBM),
            pl.BlockSpec(memory_space=pltpu.VMEM),
            pl.BlockSpec(memory_space=pltpu.HBM),
            pl.BlockSpec(memory_space=pltpu.HBM),
        ],
        out_specs=[pl.BlockSpec(memory_space=pl.ANY)] * 2,
        scratch_shapes=scratch,
        compiler_params=pltpu.CompilerParams(
            collective_id=0, has_side_effects=True, vmem_limit_bytes=VMEM_LIMIT
        ),
        name="relay",
    )(activations, cotangent, gain_rows, w_up, w_down)


def inverse_root(matrix):
    low = jnp.bfloat16
    order = matrix.shape[-1]
    on_diagonal = lax.broadcasted_iota(jnp.int32, (order, order), 0) == lax.broadcasted_iota(
        jnp.int32, (order, order), 1
    )
    identity = jnp.where(on_diagonal, 1.0, 0.0).astype(jnp.float32)
    shifted = matrix + ridge_shift * identity
    norm_sq = jnp.sum(jnp.sum(shifted * shifted, axis=1, keepdims=True), axis=0, keepdims=True)
    factor = 2.5 / jnp.sqrt(norm_sq)
    moment = factor * shifted
    moment_low = moment.astype(low)
    moment_sq = matmul(moment_low, moment_low)
    square = (1.5625 * identity - 0.625 * moment + 0.0625 * moment_sq).astype(low)
    stepped = (1.25 * moment - 0.25 * moment_sq).astype(low)
    third = matmul(square, stepped).astype(low)
    fifth = matmul(square, third)
    scale = jnp.sqrt(jnp.sqrt(factor))
    return scale * (1.5625 * identity - 0.3125 * moment - 0.25 * fifth)


def gram(values, dim):
    middle = values.shape[0] // 2
    first = values[:middle] if dim == 1 else values[:, :middle]
    second = values[middle:] if dim == 1 else values[:, middle:]
    top = matmul(first, values, dim, dim)
    low_left = top[:, middle:].T
    return jnp.concatenate(
        [top, jnp.concatenate([low_left, matmul(second, second, dim, dim)], axis=1)], axis=0
    )


def precondition(hidden, grads, grams_and_roots, owner_slot, eighth, refresh_phase, block_cols):
    slots = grams_and_roots[0].shape[0]
    tokens, shard_ff = hidden.shape
    width = grads.shape[2]
    block_rows = shard_ff // BLK
    scale = 1.0 / math.sqrt(tokens)
    pieces = max(BLK // width, 1)
    per = max(width // BLK, 1)

    def kernel(
        owner_ref, eighth_ref, phase_ref, hid_ref, grad_ref, gl_ref, gr_ref, rl_ref, rr_ref,
        gl_out, gr_out, rl_out, rr_out, up_out,
        hid, dy, gl, gr, rl, rr, block, due, sem,
    ):
        slot = pl.program_id(0)

        def loads(at):
            row, col = lax.div(block[at], block_cols), lax.rem(block[at], block_cols)
            copy = lambda src, dst, n: pltpu.make_async_copy(src, dst, sem.at[at, n])
            copies = [
                copy(hid_ref.at[:, pl.ds(pl.multiple_of(row * BLK, BLK), BLK)], hid.at[at], 0)
            ]
            if width >= BLK:
                first = pl.multiple_of(lax.rem(col, per) * BLK, BLK)
                source = grad_ref.at[lax.div(col, per), :, pl.ds(first, BLK)]
                copies.append(copy(source, dy.at[at], 1))
            else:
                for piece in range(pieces):
                    target = dy.at[at, :, pl.ds(piece * width, width)]
                    copies.append(copy(grad_ref.at[col * pieces + piece], target, 1 + piece))
            sources = ((gl_ref, gl), (gr_ref, gr), (rl_ref, rl), (rr_ref, rr))
            for n, (source, target) in enumerate(sources):
                copies.append(copy(source.at[at], target.at[at], 1 + pieces + n))
            return copies

        @pl.when(slot == 0)
        def _():
            section, mp_no = lax.axis_index("section"), lax.axis_index("mp")
            base = (lax.axis_index("dp") * lax.axis_size("mp") + mp_no) * slots
            phase = lax.rem(phase_ref[0], 8)

            for at in range(block_rows * block_cols):
                row, col = mp_no * block_rows + at // block_cols, at % block_cols
                place = owner_ref[section, col, row] - base
                place = jnp.where((place >= 0) & (place < slots), place, slots)
                block[place] = at
                due[place] = jnp.where(eighth_ref[section, col, row] == phase, 1, 0)

            @pl.loop(0, slots)
            def _(at):
                for copy in loads(at):
                    copy.start()

        copies = loads(slot)
        for copy in copies[: 1 + pieces]:
            copy.wait()
        grad_low = (matmul(hid[slot], dy[slot], 0, 0) * scale).astype(jnp.bfloat16)
        for copy in copies[1 + pieces :]:
            copy.wait()
        gl_out[0] = decay_rate * gl[slot] + gram(grad_low, 1) * (1.0 / BLK)
        gr_out[0] = decay_rate * gr[slot] + gram(grad_low, 0) * (1.0 / BLK)

        @pl.when(due[slot] != 0)
        def _():
            rl_out[0] = inverse_root(gl_out[0]).astype(jnp.bfloat16)
            rr_out[0] = inverse_root(gr_out[0]).astype(jnp.bfloat16)

        @pl.when(due[slot] == 0)
        def _():
            rl_out[0] = rl[slot]
            rr_out[0] = rr[slot]

        right_part = matmul(grad_low, rr_out[0]).astype(jnp.bfloat16)
        up_out[0] = matmul(rl_out[0], right_part).astype(jnp.bfloat16)

    low, f32 = jnp.bfloat16, jnp.float32
    square_spec = pl.BlockSpec((1, BLK, BLK), lambda s: (s, 0, 0))
    square = lambda dtype: jax.ShapeDtypeStruct((slots, BLK, BLK), dtype)
    return pl.pallas_call(
        kernel,
        grid=(slots,),
        in_specs=[pl.BlockSpec(memory_space=pltpu.SMEM)] * 3
        + [pl.BlockSpec(memory_space=pl.ANY)] * 6,
        out_specs=[square_spec] * 5,
        out_shape=[square(f32), square(f32), square(low), square(low), square(low)],
        scratch_shapes=[
            pltpu.VMEM((slots, tokens, BLK), low),
            pltpu.VMEM((slots, tokens, BLK), low),
            pltpu.VMEM((slots, BLK, BLK), f32),
            pltpu.VMEM((slots, BLK, BLK), f32),
            pltpu.VMEM((slots, BLK, BLK), low),
            pltpu.VMEM((slots, BLK, BLK), low),
            pltpu.SMEM((slots + 1,), jnp.int32),
            pltpu.SMEM((slots + 1,), jnp.int32),
            pltpu.SemaphoreType.DMA((slots, 5 + pieces)),
        ],
        compiler_params=pltpu.CompilerParams(
            dimension_semantics=("arbitrary",), vmem_limit_bytes=VMEM_LIMIT
        ),
        name="precondition",
    )(owner_slot, eighth, refresh_phase, hidden, grads, *grams_and_roots)


def on_device(
    activations,
    cotangent,
    norm_gain,
    w_up,
    w_down,
    gram_left,
    gram_right,
    root_left,
    root_right,
    owner_slot,
    eighth,
    refresh_phase,
):
    width, shard_ff = w_up.shape[1:]
    hidden, grads = relay(activations, cotangent, norm_gain, w_up[0], w_down[0])
    results = precondition(
        hidden.reshape(-1, shard_ff),
        grads.reshape(grads.shape[0], -1, width),
        [x[0] for x in (gram_left, gram_right, root_left, root_right)],
        owner_slot.swapaxes(1, 2),
        eighth.swapaxes(1, 2),
        refresh_phase,
        activations.shape[2] // BLK,
    )
    return tuple(result[None] for result in results)


def solution(mesh):
    return jax.shard_map(
        on_device,
        mesh=mesh,
        in_specs=(
            P(None, "dp", None),
            P(None, "dp", None),
            P("section", None),
            P("section", "dp", "mp"),
            P("section", "dp", "mp"),
            P("section", ("dp", "mp"), None, None),
            P("section", ("dp", "mp"), None, None),
            P("section", ("dp", "mp"), None, None),
            P("section", ("dp", "mp"), None, None),
            P(),
            P(),
            P(),
        ),
        out_specs=(
            P("section", ("dp", "mp"), None, None),
            P("section", ("dp", "mp"), None, None),
            P("section", ("dp", "mp"), None, None),
            P("section", ("dp", "mp"), None, None),
            P("section", ("dp", "mp"), None, None),
        ),
        check_vma=False,
    )
```
